256 devices in a mesh: dp: 64 (over y, z, core), mp: 4 (over x).
Axes of the slice: x: 4, y: 4, z: 8, core: 2. Of those that a mesh axis runs over, the one named last changes fastest.
Arguments:
- seg_queries: bfloat16 [64, 256, 3072], P('dp', None, 'mp'), may hold values from -6 to 6
- seg_keys: bfloat16 [64, 256, 3072], P('dp', None, 'mp'), may hold values from -6 to 6
- seg_values: bfloat16 [64, 256, 3072], P('dp', None, 'mp'), may hold values from -8 to 8
- memory_keys: bfloat16 [64, 256, 3072], P('dp', None, 'mp'), may hold values from -4 to 4
- memory_values: bfloat16 [64, 256, 3072], P('dp', None, 'mp'), may hold values from -8 to 8
- new_owner: int32 [64], replicated, may hold values from 0 to 63, each once
- kept_blocks: int32 [64], replicated, may hold values from 1 to 2, 96 in all
- rel_bias: float32 [24, 512], P('mp'), may hold values from -5 to 5
- norm_gain: float32 [3072], P('mp'), may hold values from 0.5 to 1.5
- cotangent: bfloat16 [64, 256, 3072], P('dp', None, 'mp'), may hold values from -8 to 8
Outputs:
- attended: bfloat16 [64, 256, 3072], P('dp', None, 'mp')
- query_grad: bfloat16 [64, 256, 3072], P('dp', None, 'mp')
- key_grad: bfloat16 [64, 256, 3072], P('dp', None, 'mp')
- value_grad: bfloat16 [64, 256, 3072], P('dp', None, 'mp')
- bias_grad: float32 [24, 512], P('mp', 'dp')
- gain_grad: float32 [3072], P('mp')
The draws below stay inside these ranges and needn't reach their ends.
Inputs may be any that keep to these rules, and one draw needn't show every extreme that they name: `new_owner`: each old slot's stream goes to one device, and every device takes exactly one stream. A slot keeps its most recent kept_blocks blocks of 128 memory positions; some slot keeps all 2.
All inputs are finite; a program needn't handle non-finite values.
Results may differ from the reference program's by a relative error of at most 0.018.
Values may be sent and summed in bfloat16 or wider, within the bound.
No kernel may reach another device: no remote copies, remote signals or barrier semaphores. Data moves between devices by JAX's collectives and lax.ppermute only.
A program may use at most 64 MiB of HBM per device.

```python
import math
import jax
import jax.numpy as jnp
import numpy as np
from jax import lax

HEADS = 24
DH = 128
SEG = 256
MEM = 256
BLOCK = 128
MEM_BLOCKS = 2
POS = 512
HD = 3072
STREAMS = 64
N_DP = 64


def base_field(key, shape):
    return jnp.clip(jax.random.normal(key, shape, jnp.float32), -4.0, 4.0)


def head_ramp():
    head_ids = (jnp.arange(HD) // DH).astype(jnp.float32)
    return 0.6 * 3.0 ** (head_ids / max(HEADS - 1, 1))


def draw_seg_queries(key, part):
    sample = base_field(jax.random.fold_in(key, 1), (STREAMS, SEG, HD))
    return sample.astype(jnp.bfloat16)


def draw_memory_keys(key, part):
    sample = base_field(jax.random.fold_in(key, 2), (STREAMS, MEM, HD))
    return sample.astype(jnp.bfloat16)


def draw_seg_values(key, part):
    sample = base_field(jax.random.fold_in(key, 3), (STREAMS, SEG, HD)) * head_ramp()
    return sample.astype(jnp.bfloat16)


def draw_memory_values(key, part):
    sample = base_field(jax.random.fold_in(key, 4), (STREAMS, MEM, HD)) * head_ramp()
    return sample.astype(jnp.bfloat16)


def draw_cotangent(key, part):
    stream_ids = jnp.arange(STREAMS).astype(jnp.float32)[:, None, None]
    sample = base_field(jax.random.fold_in(key, 5), (STREAMS, SEG, HD))
    factor = 0.5 * 3.0 ** (stream_ids / max(STREAMS - 1, 1))
    sample = sample * factor
    return sample.astype(jnp.bfloat16)


def levels(key, dims, split, low, largest):
    factor_of, own = 1.0, jax.random.fold_in(key, 6)
    for position, blocks in split:
        draws = jnp.exp(jax.random.uniform(jax.random.fold_in(own, position), (blocks,), jnp.float32, low / len(split), largest / len(split)))
        factor_of = factor_of * jnp.repeat(draws, dims[position] // blocks).reshape([-1 if axis == position else 1 for axis in range(len(dims))])
    return factor_of


def profile(number_of, total, limit, skew):
    weights = [(1 << 20) // math.isqrt(grade ** skew) + 1 for grade in range(2, number_of + 1)]
    surplus, given = total - limit - (number_of - 1), [1] * (number_of - 1)
    while surplus > 0:
        candidates = [i for i in range(number_of - 1) if given[i] < limit]
        pool, budget = sum([weights[i] for i in candidates]), surplus
        for i in candidates:
            addition = min(limit - given[i], max(1, budget * weights[i] // pool), surplus)
            given[i] = given[i] + addition
            surplus = surplus - addition
    return np.array([limit] + given)


def ragged_sizes(rng, amount, total, most, slope):
    if amount == 2:
        one = jax.random.randint(rng, (), max(1, total - most), min(most, total - 1) + 1)
        return jnp.stack([one, total - one])
    lengths = jnp.asarray(profile(amount, total, most, slope), jnp.int32)
    twos = (amount - 1) // 2
    donor, taker = lengths[1:1 + 2 * twos:2], lengths[2:2 + 2 * twos:2]
    room = jnp.minimum(donor - 1, most - taker)
    moved = jax.random.randint(jax.random.fold_in(rng, 1), (twos,), 0, 1 << 20) % (room + 1)
    lengths = lengths.at[1:1 + 2 * twos:2].set(donor - moved).at[2:2 + 2 * twos:2].set(taker + moved)
    return lengths[jax.random.permutation(jax.random.fold_in(rng, 2), amount)]


def gaussian(stream_key, shape, scale, most, cuts=(), kind=jnp.bfloat16):
    factor_of = levels(stream_key, shape, cuts, -0.22, 0.18) if cuts else 1.0
    values = jax.random.normal(stream_key, shape, jnp.float32) * scale * factor_of
    return jnp.minimum(jnp.maximum(values, -most), most).astype(kind)


def setup_inputs(seed: int = 0) -> dict:
    arg_keys = jax.random.split(jax.random.key(seed), 11)
    seg_queries = draw_seg_queries(jax.random.fold_in(arg_keys[10], 71), 0)
    seg_keys = gaussian(arg_keys[1], (STREAMS, SEG, HD), 1.0, 6.0, ((0, 64), (2, 4)))
    seg_values = draw_seg_values(jax.random.fold_in(arg_keys[10], 71), 0)
    memory_keys = draw_memory_keys(jax.random.fold_in(arg_keys[10], 71), 0)
    memory_values = draw_memory_values(jax.random.fold_in(arg_keys[10], 71), 0)
    new_owner = jax.random.permutation(arg_keys[5], STREAMS).astype(jnp.int32)
    kept_blocks = ragged_sizes(arg_keys[6], STREAMS, N_DP * (MEM_BLOCKS + 1) // 2, MEM_BLOCKS, 2).astype(jnp.int32)
    rel_bias = gaussian(arg_keys[7], (HEADS, POS), 1.0, 5.0, ((0, 4),), jnp.float32)
    norm_gain = jnp.clip(1.0 + 0.1 * jax.random.normal(arg_keys[8], (HD,), jnp.float32), 0.5, 1.5)
    cotangent = draw_cotangent(jax.random.fold_in(arg_keys[10], 71), 0)
    return {"seg_queries": seg_queries, "seg_keys": seg_keys, "seg_values": seg_values, "memory_keys": memory_keys, "memory_values": memory_values, "new_owner": new_owner, "kept_blocks": kept_blocks, "rel_bias": rel_bias, "norm_gain": norm_gain, "cotangent": cotangent}


def reference(seg_queries, seg_keys, seg_values, memory_keys, memory_values, new_owner, kept_blocks, rel_bias, norm_gain, cotangent):
    slot_ids = jnp.arange(STREAMS, dtype=jnp.int32)
    source = jnp.zeros((STREAMS,), jnp.int32).at[new_owner].set(slot_ids)
    score_scale = DH ** (-0.5)
    query_pos = jnp.arange(SEG, dtype=jnp.int32)[:, None]
    key_pos = jnp.arange(POS, dtype=jnp.int32)[None, :]
    distance = MEM + query_pos - key_pos
    dist_index = jnp.clip(distance, 0, POS - 1).astype(jnp.int32)
    bias_matrix = rel_bias[:, dist_index]

    def one_stream(stream):
        anchor = source[stream]
        kept_here = kept_blocks[anchor]
        query_heads = seg_queries[stream].astype(jnp.float32).reshape(SEG, HEADS, DH)
        key_heads = jnp.concatenate([memory_keys[anchor], seg_keys[stream]], axis=0).astype(jnp.float32).reshape(POS, HEADS, DH)
        value_heads = jnp.concatenate([memory_values[anchor], seg_values[stream]], axis=0).astype(jnp.float32).reshape(POS, HEADS, DH)
        allowed = (distance >= 0) & (key_pos >= MEM - BLOCK * kept_here)
        scores = jnp.einsum('ihd,jhd->hij', query_heads, key_heads) * score_scale + bias_matrix
        row_max = lax.optimization_barrier(jnp.max(jnp.where(allowed, scores, -1e+30), axis=-1, keepdims=True))
        unnormed = jnp.where(allowed, jnp.exp(scores - row_max), 0.0)
        weights_f = unnormed / lax.optimization_barrier(jnp.sum(unnormed, axis=-1, keepdims=True))
        weights_b = lax.optimization_barrier(weights_f.astype(jnp.bfloat16)).astype(jnp.float32)
        out_heads = jnp.einsum('hij,jhd->ihd', weights_b, value_heads)
        attn_out = out_heads.reshape(SEG, HD)
        inv_rms = lax.rsqrt(lax.optimization_barrier(jnp.sum(attn_out * attn_out, axis=1)) / HD + 1e-06)
        attended = (attn_out * inv_rms[:, None] * norm_gain).astype(jnp.bfloat16)
        upstream = cotangent[stream].astype(jnp.float32)
        gain_cot = upstream * norm_gain
        cross_sum = lax.optimization_barrier(jnp.sum(gain_cot * attn_out, axis=1))
        out_grad = (inv_rms[:, None] * gain_cot - attn_out * (inv_rms ** 3 * cross_sum / HD)[:, None]).astype(jnp.bfloat16)
        grad_heads = lax.optimization_barrier(out_grad).astype(jnp.float32).reshape(SEG, HEADS, DH)
        row_delta = jnp.einsum('ihd,ihd->hi', grad_heads, out_heads)
        prob_grad = jnp.einsum('ihd,jhd->hij', grad_heads, value_heads)
        score_grad = weights_f * (prob_grad - row_delta[:, :, None])
        score_grad_b = lax.optimization_barrier(score_grad.astype(jnp.bfloat16)).astype(jnp.float32)
        query_grad = (jnp.einsum('hij,jhd->ihd', score_grad_b, key_heads) * score_scale).reshape(SEG, HD).astype(jnp.bfloat16)
        key_grad = (jnp.einsum('hij,ihd->jhd', score_grad_b[:, :, MEM:], query_heads) * score_scale).reshape(SEG, HD).astype(jnp.bfloat16)
        value_grad = jnp.einsum('hij,ihd->jhd', weights_b[:, :, MEM:], grad_heads).reshape(SEG, HD).astype(jnp.bfloat16)
        local_bias = jnp.zeros((HEADS, POS), jnp.float32).at[:, dist_index].add(jnp.where(allowed, score_grad, 0.0))
        local_gain = lax.optimization_barrier(jnp.sum(upstream * attn_out * inv_rms[:, None], axis=0))
        return (attended, query_grad, key_grad, value_grad, local_bias, local_gain)
    results = lax.map(one_stream, slot_ids)
    return (results[0], results[1], results[2], results[3], lax.optimization_barrier(jnp.sum(results[4], axis=0)), lax.optimization_barrier(jnp.sum(results[5], axis=0)))
```

```python
import math

import jax
import jax.numpy as jnp
from jax import lax
from jax.experimental import pallas as pl
from jax.experimental.pallas import tpu as pltpu
from jax.sharding import PartitionSpec as P

DH = 128
BLOCK = 128
HD = 3072
SEG = 256
MEM = 256
POS = 512
HEADS = 6
COLS = HEADS * DH
DP = 64
PIECE = (2 * MEM) // DP
LOG2E = math.log2(math.e)
SCALE = DH ** (-0.5)
NT = (((1,), (1,)), ((), ()))
NN = (((1,), (0,)), ((), ()))
TN = (((0,), (0,)), ((), ()))


def dot(a, b, dims):
    return lax.dot_general(a, b, dims, preferred_element_type=jnp.float32)


def roll(x, shift):
    shift = shift % x.shape[1]
    return x if shift == 0 else pltpu.roll(x, shift, axis=1)


def reverse_lanes(x):
    rows, width = x.shape
    index = 127 - lax.broadcasted_iota(jnp.int32, (rows, 128), 1)
    parts = [
        jnp.take_along_axis(x[:, start : start + 128], index, axis=1)
        for start in range(width - 128, -1, -128)
    ]
    return jnp.concatenate(parts, axis=1)


def by_distance(x):
    return roll(reverse_lanes(x), -255)


def stagger(x, unit):
    row = lax.broadcasted_iota(jnp.int32, x.shape, 0)
    for bit in (1, 2, 4):
        x = jnp.where((row & bit) != 0, roll(x, bit * unit), x)
    return x


def bias_rows(table_row):
    base = stagger(jnp.broadcast_to(by_distance(jnp.broadcast_to(table_row, (8, POS))), (8, POS)), 1)
    return jnp.concatenate([roll(base, 8 * group) for group in range(SEG // 8)], axis=0)


def diagonal_row(score_grad):
    level = [score_grad[8 * g : 8 * g + 8] for g in range(SEG // 8)]
    shift = 8
    while len(level) > 1:
        level = [level[k] + roll(level[k + 1], -shift) for k in range(0, len(level), 2)]
        shift *= 2
    return jnp.sum(stagger(level[0], -1), axis=0, keepdims=True)


def reorder_kernel(owner_ref, in_ref, out_ref):
    for slot in range(DP):
        out_ref[owner_ref[slot]] = in_ref[slot]


def reorder(new_owner, pieces):
    return pl.pallas_call(
        reorder_kernel,
        out_shape=jax.ShapeDtypeStruct(pieces.shape, pieces.dtype),
        in_specs=[
            pl.BlockSpec(memory_space=pltpu.SMEM),
            pl.BlockSpec(memory_space=pltpu.VMEM),
        ],
        out_specs=pl.BlockSpec(memory_space=pltpu.VMEM),
        name="reorder",
    )(new_owner, pieces)


def forward_kernel(
    kept_ref, q_ref, ks_ref, vs_ref, mem_ref, bias_ref, cot_ref, gain_ref,
    out_ref, prob_ref, stats_ref, square_ref, cross_ref,
):
    head = pl.program_id(0)
    q = q_ref[0]
    bias = bias_rows(bias_ref[pl.ds(head, 1), :] * LOG2E)
    factor = SCALE * LOG2E
    s_mem = dot(q, mem_ref[:MEM], NT) * factor + bias[:, :MEM]
    s_seg = dot(q, ks_ref[0], NT) * factor + bias[:, MEM:]
    col = lax.broadcasted_iota(jnp.int32, (SEG, MEM), 1)
    row = lax.broadcasted_iota(jnp.int32, (SEG, MEM), 0)
    s_mem = jnp.where(col >= MEM - BLOCK * kept_ref[0], s_mem, -1e30)
    s_seg = jnp.where(col <= row, s_seg, -1e30)
    top = jnp.maximum(
        jnp.max(s_mem, axis=1, keepdims=True), jnp.max(s_seg, axis=1, keepdims=True)
    )
    p_mem = jnp.exp2(s_mem - top)
    p_seg = jnp.exp2(s_seg - top)
    total = jnp.sum(p_mem, axis=1, keepdims=True) + jnp.sum(p_seg, axis=1, keepdims=True)
    inverse = 1.0 / total
    w_mem = (p_mem * inverse).astype(jnp.bfloat16)
    w_seg = (p_seg * inverse).astype(jnp.bfloat16)
    prob_ref[0, :, :MEM] = w_mem
    prob_ref[0, :, MEM:] = w_seg
    out = dot(w_mem, mem_ref[MEM:], NN) + dot(w_seg, vs_ref[0], NN)
    out_ref[...] = out
    square = out * out
    cross = cot_ref[0].astype(jnp.float32) * gain_ref[...] * out

    @pl.when(head == 0)
    def _():
        square_ref[...] = square
        cross_ref[...] = cross

    @pl.when(head > 0)
    def _():
        square_ref[...] += square
        cross_ref[...] += cross

    @pl.when(head == HEADS - 1)
    def _():
        stats_ref[...] = jnp.zeros((8, SEG), jnp.float32)
        stats_ref[0:1, :] = jnp.sum(square_ref[...].T, axis=0, keepdims=True)
        stats_ref[1:2, :] = jnp.sum(cross_ref[...].T, axis=0, keepdims=True)


def column_spec():
    return pl.BlockSpec((1, SEG, DH), lambda h: (0, 0, h))


def whole(shape):
    return pl.BlockSpec(shape, lambda h: (0,) * len(shape))


def forward(kept, q, ks, vs, mem, bias, cot, gain):
    return pl.pallas_call(
        forward_kernel,
        grid=(HEADS,),
        out_shape=(
            jax.ShapeDtypeStruct((SEG, COLS), jnp.float32),
            jax.ShapeDtypeStruct((HEADS, SEG, POS), jnp.bfloat16),
            jax.ShapeDtypeStruct((8, SEG), jnp.float32),
        ),
        in_specs=[
            pl.BlockSpec(memory_space=pltpu.SMEM),
            column_spec(),
            column_spec(),
            column_spec(),
            pl.BlockSpec((2 * MEM, DH), lambda h: (0, h)),
            whole((HEADS, POS)),
            column_spec(),
            pl.BlockSpec((1, DH), lambda h: (0, h)),
        ],
        out_specs=(
            pl.BlockSpec((SEG, DH), lambda h: (0, h)),
            pl.BlockSpec((1, SEG, POS), lambda h: (h, 0, 0)),
            whole((8, SEG)),
        ),
        scratch_shapes=[
            pltpu.VMEM((SEG, DH), jnp.float32),
            pltpu.VMEM((SEG, DH), jnp.float32),
        ],
        compiler_params=pltpu.CompilerParams(vmem_limit_bytes=48 << 20),
        name="forward",
    )(kept, q, ks, vs, mem, bias, cot, gain)


def backward_kernel(
    stats0_ref, stats1_ref, stats2_ref, stats3_ref,
    q_ref, ks_ref, vs_ref, mem_ref, cot_ref, gain_ref, attn_ref, prob_ref,
    attended_ref, dq_ref, dk_ref, dv_ref, share_ref,
    inv_ref, coef_ref, gain_sum_ref, diag_ref,
):
    head = pl.program_id(0)

    @pl.when(head == 0)
    def _():
        stats = (stats0_ref[...] + stats1_ref[...]) + (stats2_ref[...] + stats3_ref[...])
        inv = lax.rsqrt(stats[0:1] / HD + 1e-06)
        coef = inv * inv * inv * stats[1:2] / HD
        inv_ref[...] = jnp.broadcast_to(inv, (DH, SEG)).T
        coef_ref[...] = jnp.broadcast_to(coef, (DH, SEG)).T
        gain_sum_ref[...] = jnp.zeros((8, DH), jnp.float32)
        diag_ref[...] = jnp.zeros((8, POS), jnp.float32)

    q = q_ref[0]
    attn = attn_ref[...]
    inv = inv_ref[...]
    gain = gain_ref[...]
    upstream = cot_ref[0].astype(jnp.float32)
    normed = attn * inv
    attended_ref[0] = (normed * gain).astype(jnp.bfloat16)
    gain_sum_ref[pl.ds(head, 1), :] = jnp.sum(upstream * normed, axis=0, keepdims=True)
    out_grad = (inv * (upstream * gain) - attn * coef_ref[...]).astype(jnp.bfloat16)
    delta = jnp.sum(out_grad.astype(jnp.float32) * attn, axis=1, keepdims=True)
    w_mem = prob_ref[0, :, :MEM]
    w_seg = prob_ref[0, :, MEM:]
    dp_mem = dot(out_grad, mem_ref[MEM:], NT)
    dp_seg = dot(out_grad, vs_ref[0], NT)
    ds_mem = w_mem.astype(jnp.float32) * (dp_mem - delta)
    ds_seg = w_seg.astype(jnp.float32) * (dp_seg - delta)
    dsb_mem = ds_mem.astype(jnp.bfloat16)
    dsb_seg = ds_seg.astype(jnp.bfloat16)
    dq_ref[0] = (
        (dot(dsb_mem, mem_ref[:MEM], NN) + dot(dsb_seg, ks_ref[0], NN)) * SCALE
    ).astype(jnp.bfloat16)
    dk_ref[0] = (dot(dsb_seg, q, TN) * SCALE).astype(jnp.bfloat16)
    dv_ref[0] = dot(w_seg, out_grad, TN).astype(jnp.bfloat16)
    diag_ref[pl.ds(head, 1), :] = diagonal_row(jnp.concatenate([ds_mem, ds_seg], axis=1))

    @pl.when(head == HEADS - 1)
    def _():
        bias = stagger(by_distance(diag_ref[...]), 8)
        bias = jnp.concatenate([bias, bias[:, :128]], axis=1)
        lane = lax.broadcasted_iota(jnp.int32, (8, DH), 1)
        row = lax.broadcasted_iota(jnp.int32, (8, DH), 0)
        own = (lane >= 8 * row) & (lane < 8 * row + 8) & (row < HEADS)
        gains = gain_sum_ref[...]
        for dest in range(DP):
            start, shift = divmod(8 * dest, 128)
            here = bias[:, 128 * start : 128 * start + 128]
            after = bias[:, 128 * start + 128 : 128 * start + 256]
            part = jnp.where(lane < 128 - shift, roll(here, -shift), roll(after, -shift))
            part = jnp.sum(jnp.where(own, part, 0.0), axis=0, keepdims=True)
            share_ref[dest] = jnp.where(row == HEADS, part, gains)


def backward(stats, q, ks, vs, mem, cot, gain, attn, prob):
    big = jax.ShapeDtypeStruct((1, SEG, COLS), jnp.bfloat16)
    return pl.pallas_call(
        backward_kernel,
        grid=(HEADS,),
        out_shape=(big, big, big, big, jax.ShapeDtypeStruct((DP, 8, DH), jnp.float32)),
        in_specs=[
            whole((8, SEG)),
            whole((8, SEG)),
            whole((8, SEG)),
            whole((8, SEG)),
            column_spec(),
            column_spec(),
            column_spec(),
            pl.BlockSpec((2 * MEM, DH), lambda h: (0, h)),
            column_spec(),
            pl.BlockSpec((1, DH), lambda h: (0, h)),
            pl.BlockSpec((SEG, DH), lambda h: (0, h)),
            pl.BlockSpec((1, SEG, POS), lambda h: (h, 0, 0)),
        ],
        out_specs=(
            column_spec(),
            column_spec(),
            column_spec(),
            column_spec(),
            whole((DP, 8, DH)),
        ),
        scratch_shapes=[
            pltpu.VMEM((SEG, DH), jnp.float32),
            pltpu.VMEM((SEG, DH), jnp.float32),
            pltpu.VMEM((8, DH), jnp.float32),
            pltpu.VMEM((8, POS), jnp.float32),
        ],
        compiler_params=pltpu.CompilerParams(vmem_limit_bytes=48 << 20),
        name="backward",
    )(*stats, q, ks, vs, mem, cot, gain, attn, prob)


def collect_kernel(share_ref, bias_ref, gain_ref):
    total = jnp.sum(share_ref[...], axis=0)
    gain_ref[...] = total[:HEADS]
    bias = stagger(jnp.broadcast_to(total[HEADS : HEADS + 1], (8, DH)), -8)
    bias_ref[...] = bias[:HEADS, :8]


def collect(shares):
    return pl.pallas_call(
        collect_kernel,
        out_shape=(
            jax.ShapeDtypeStruct((HEADS, 8), jnp.float32),
            jax.ShapeDtypeStruct((HEADS, DH), jnp.float32),
        ),
        name="collect",
    )(shares)


def exchange(x):
    return lax.all_to_all(x, "dp", split_axis=0, concat_axis=0, tiled=True)


def body(
    seg_queries, seg_keys, seg_values, memory_keys, memory_values,
    new_owner, kept_blocks, rel_bias, norm_gain, cotangent,
):
    own_index = lax.axis_index("dp")
    kept = jnp.sum(jnp.where(new_owner == own_index, kept_blocks, 0)).reshape(1)
    gain = norm_gain.reshape(1, COLS)
    pieces = jnp.concatenate([memory_keys[0], memory_values[0]], axis=0)
    spread = exchange(pieces.reshape(DP, PIECE, COLS))
    mem = exchange(reorder(new_owner, spread)).reshape(2 * MEM, COLS)
    attn, prob, stats = forward(
        kept, seg_queries, seg_keys, seg_values, mem, rel_bias, cotangent, gain
    )
    others = [
        lax.ppermute(stats, "mp", [(i, (i + step) % 4) for i in range(4)]) for step in (1, 2, 3)
    ]
    attended, query_grad, key_grad, value_grad, shares = backward(
        [stats] + others, seg_queries, seg_keys, seg_values, mem, cotangent, gain, attn, prob
    )
    bias_grad, gain_grad = collect(exchange(shares))
    return attended, query_grad, key_grad, value_grad, bias_grad, gain_grad.reshape(COLS)


def solution(mesh):
    row = P("dp", None, "mp")
    return jax.shard_map(
        body,
        mesh=mesh,
        in_specs=(row, row, row, row, row, P(), P(), P("mp", None), P("mp"), row),
        out_specs=(row, row, row, row, P("mp", "dp"), P("mp")),
        check_vma=False,
    )
```

```python
import math

import jax
import jax.numpy as jnp
from jax import lax
from jax.experimental import pallas as pl
from jax.experimental.pallas import tpu as pltpu
from jax.sharding import PartitionSpec as P

DH = 128
BLOCK = 128
HD = 3072
SEG = 256
MEM = 256
POS = 512
HEADS = 6
COLS = HEADS * DH
DP = 64
PIECE = (2 * MEM) // DP
LOG2E = math.log2(math.e)
SCALE = DH ** (-0.5)
FACTOR = SCALE * LOG2E
GROUP = 2
STEPS = HEADS // GROUP
NT = (((1,), (1,)), ((), ()))
NN = (((1,), (0,)), ((), ()))
TN = (((0,), (0,)), ((), ()))


def dot(a, b, dims):
    return lax.dot_general(a, b, dims, preferred_element_type=jnp.float32)


def roll(x, shift):
    shift = shift % x.shape[1]
    return x if shift == 0 else pltpu.roll(x, shift, axis=1)


def reverse_lanes(x):
    rows, width = x.shape
    index = 127 - lax.broadcasted_iota(jnp.int32, (rows, 128), 1)
    parts = [
        jnp.take_along_axis(x[:, start : start + 128], index, axis=1)
        for start in range(width - 128, -1, -128)
    ]
    return jnp.concatenate(parts, axis=1)


def by_distance(x):
    return roll(reverse_lanes(x), -255)


def stagger(x, unit):
    row = lax.broadcasted_iota(jnp.int32, x.shape, 0)
    for bit in (1, 2, 4):
        x = jnp.where((row & bit) != 0, roll(x, bit * unit), x)
    return x


def bias_rows(table_row):
    base = stagger(jnp.broadcast_to(by_distance(jnp.broadcast_to(table_row, (8, POS))), (8, POS)), 1)
    return jnp.concatenate([roll(base, 8 * group) for group in range(SEG // 8)], axis=0)


def diagonal_row(score_grad):
    level = [score_grad[8 * g : 8 * g + 8] for g in range(SEG // 8)]
    shift = 8
    while len(level) > 1:
        level = [level[k] + roll(level[k + 1], -shift) for k in range(0, len(level), 2)]
        shift *= 2
    return jnp.sum(stagger(level[0], -1), axis=0, keepdims=True)


def reorder_kernel(owner_ref, in_ref, out_ref):
    for slot in range(DP):
        out_ref[owner_ref[slot]] = in_ref[slot]


def reorder(new_owner, pieces):
    return pl.pallas_call(
        reorder_kernel,
        out_shape=jax.ShapeDtypeStruct(pieces.shape, pieces.dtype),
        in_specs=[
            pl.BlockSpec(memory_space=pltpu.SMEM),
            pl.BlockSpec(memory_space=pltpu.VMEM),
        ],
        out_specs=pl.BlockSpec(memory_space=pltpu.VMEM),
        name="reorder",
    )(new_owner, pieces)


def segment_kernel(
    kept_ref, q_ref, ks_ref, vs_ref, bias_ref,
    prob_ref, out_ref, top_ref, total_ref, mem_bias_ref,
):
    col = lax.broadcasted_iota(jnp.int32, (SEG, MEM), 1)
    row = lax.broadcasted_iota(jnp.int32, (SEG, MEM), 0)
    ones = jnp.ones((SEG, DH), jnp.bfloat16)
    for g in range(GROUP):
        head = pl.program_id(0) * GROUP + g
        cols = slice(DH * g, DH * g + DH)
        bias = bias_rows(bias_ref[pl.ds(head, 1), :] * LOG2E)
        mem_bias_ref[g] = jnp.where(col >= MEM - BLOCK * kept_ref[0], bias[:, :MEM], -1e30)
        scores = dot(q_ref[0, :, cols], ks_ref[0, :, cols], NT) * FACTOR + bias[:, MEM:]
        scores = jnp.where(col <= row, scores, -1e30)
        top = jnp.max(scores, axis=1, keepdims=True)
        prob = jnp.exp2(scores - top).astype(jnp.bfloat16)
        prob_ref[g] = prob
        both = dot(prob, jnp.concatenate([vs_ref[0, :, cols], ones], axis=1), NN)
        out_ref[:, cols] = both[:, :DH]
        total_ref[:, cols] = both[:, DH:]
        top_ref[:, cols] = jnp.broadcast_to(top, (SEG, DH))


def forward_kernel(
    q_ref, mem_ref, mem_bias_ref, cot_ref, gain_ref, seg_out_ref, seg_top_ref, seg_total_ref,
    out_ref, prob_ref, factor_mem_ref, factor_seg_ref, stats_ref, square_ref, cross_ref,
):
    step = pl.program_id(0)
    ones = jnp.ones((MEM, DH), jnp.bfloat16)
    square = cross = None
    for g in range(GROUP):
        cols = slice(DH * g, DH * g + DH)
        scores = dot(q_ref[0, :, cols], mem_ref[:MEM, cols], NT) * FACTOR + mem_bias_ref[g]
        seg_top = seg_top_ref[:, cols]
        top = jnp.maximum(jnp.max(scores, axis=1, keepdims=True), seg_top)
        prob = jnp.exp2(scores - jnp.concatenate([top, top], axis=1)).astype(jnp.bfloat16)
        prob_ref[g] = prob
        both = dot(prob, jnp.concatenate([mem_ref[MEM:, cols], ones], axis=1), NN)
        shrink = jnp.exp2(seg_top - top)
        inverse = 1.0 / (both[:, DH:] + seg_total_ref[:, cols] * shrink)
        factor_seg = shrink * inverse
        out = both[:, :DH] * inverse + seg_out_ref[:, cols] * factor_seg
        factor_mem_ref[:, cols] = inverse
        factor_seg_ref[:, cols] = factor_seg
        out_ref[:, cols] = out
        part = cot_ref[0, :, cols].astype(jnp.float32) * gain_ref[:, cols] * out
        square = out * out if g == 0 else square + out * out
        cross = part if g == 0 else cross + part

    @pl.when(step == 0)
    def _():
        square_ref[...] = square
        cross_ref[...] = cross

    @pl.when(step > 0)
    def _():
        square_ref[...] += square
        cross_ref[...] += cross

    @pl.when(step == STEPS - 1)
    def _():
        stats_ref[...] = jnp.zeros((8, SEG), jnp.float32)
        stats_ref[0:1, :] = jnp.sum(square_ref[...].T, axis=0, keepdims=True)
        stats_ref[1:2, :] = jnp.sum(cross_ref[...].T, axis=0, keepdims=True)


def score_grad_kernel(
    stats0_ref, stats1_ref, stats2_ref, stats3_ref,
    vs_ref, mem_ref, cot_ref, gain_ref, attn_ref, prob_mem_ref, prob_seg_ref,
    factor_mem_ref, factor_seg_ref,
    ds_mem_ref, ds_seg_ref, og_seg_ref, attended_ref, share_ref,
    inv_ref, coef_ref, gain_sum_ref, diag_ref,
):
    step = pl.program_id(0)

    @pl.when(step == 0)
    def _():
        stats = (stats0_ref[...] + stats1_ref[...]) + (stats2_ref[...] + stats3_ref[...])
        inv = lax.rsqrt(stats[0:1] / HD + 1e-06)
        coef = inv * inv * inv * stats[1:2] / HD
        inv_ref[...] = jnp.broadcast_to(inv, (DH, SEG)).T
        coef_ref[...] = jnp.broadcast_to(coef, (DH, SEG)).T
        gain_sum_ref[...] = jnp.zeros((8, DH), jnp.float32)
        diag_ref[...] = jnp.zeros((8, POS), jnp.float32)

    inv = inv_ref[...]
    coef = coef_ref[...]
    for g in range(GROUP):
        head = step * GROUP + g
        cols = slice(DH * g, DH * g + DH)
        attn = attn_ref[:, cols]
        gain = gain_ref[:, cols]
        upstream = cot_ref[0, :, cols].astype(jnp.float32)
        normed = attn * inv
        attended_ref[0, :, cols] = (normed * gain).astype(jnp.bfloat16)
        gain_sum_ref[pl.ds(head, 1), :] = jnp.sum(upstream * normed, axis=0, keepdims=True)
        out_grad = inv * (upstream * gain) - attn * coef
        delta = jnp.sum(out_grad * attn, axis=1, keepdims=True)
        factor_mem = factor_mem_ref[:, cols]
        factor_seg = factor_seg_ref[:, cols]
        og_mem = (out_grad * factor_mem).astype(jnp.bfloat16)
        og_seg = (out_grad * factor_seg).astype(jnp.bfloat16)
        og_seg_ref[:, cols] = og_seg
        less_mem = delta * factor_mem
        less_seg = delta * factor_seg
        dp_mem = dot(og_mem, mem_ref[:, cols], NT) - jnp.concatenate([less_mem, less_mem], axis=1)
        dp_seg = dot(og_seg, vs_ref[0, :, cols], NT) - jnp.concatenate([less_seg, less_seg], axis=1)
        ds_mem = prob_mem_ref[g].astype(jnp.float32) * dp_mem
        ds_seg = prob_seg_ref[g].astype(jnp.float32) * dp_seg
        ds_mem_ref[g] = ds_mem.astype(jnp.bfloat16)
        ds_seg_ref[g] = ds_seg.astype(jnp.bfloat16)
        diag_ref[pl.ds(head, 1), :] = diagonal_row(jnp.concatenate([ds_mem, ds_seg], axis=1))

    @pl.when(step == STEPS - 1)
    def _():
        bias = stagger(by_distance(diag_ref[...]), 8)
        bias = jnp.concatenate([bias, bias[:, :128]], axis=1)
        lane = lax.broadcasted_iota(jnp.int32, (8, DH), 1)
        row = lax.broadcasted_iota(jnp.int32, (8, DH), 0)
        own = (lane >= 8 * row) & (lane < 8 * row + 8) & (row < HEADS)
        gains = gain_sum_ref[...]
        for dest in range(DP):
            start, shift = divmod(8 * dest, 128)
            here = bias[:, 128 * start : 128 * start + 128]
            after = bias[:, 128 * start + 128 : 128 * start + 256]
            part = jnp.where(lane < 128 - shift, roll(here, -shift), roll(after, -shift))
            part = jnp.sum(jnp.where(own, part, 0.0), axis=0, keepdims=True)
            share_ref[dest] = jnp.where(row == HEADS, part, gains).astype(share_ref.dtype)


def input_grad_kernel(
    q_ref, ks_ref, mem_ref, ds_mem_ref, ds_seg_ref, prob_seg_ref, og_seg_ref,
    dq_ref, dk_ref, dv_ref,
):
    for g in range(GROUP):
        cols = slice(DH * g, DH * g + DH)
        ds_seg = ds_seg_ref[g]
        dq = dot(ds_mem_ref[g], mem_ref[:, cols], NN) + dot(ds_seg, ks_ref[0, :, cols], NN)
        dq_ref[0, :, cols] = (dq * SCALE).astype(jnp.bfloat16)
        dk_ref[0, :, cols] = (dot(ds_seg, q_ref[0, :, cols], TN) * SCALE).astype(jnp.bfloat16)
        dv_ref[0, :, cols] = dot(prob_seg_ref[g], og_seg_ref[:, cols], TN).astype(jnp.bfloat16)


def token_spec():
    return pl.BlockSpec((1, SEG, DH * GROUP), lambda h: (0, 0, h))


def column_spec():
    return pl.BlockSpec((SEG, DH * GROUP), lambda h: (0, h))


def square_spec():
    return pl.BlockSpec((GROUP, SEG, SEG), lambda h: (h, 0, 0))


def gain_spec():
    return pl.BlockSpec((1, DH * GROUP), lambda h: (0, h))


def keys_spec():
    return pl.BlockSpec((MEM, DH * GROUP), lambda h: (0, h))


def values_spec():
    return pl.BlockSpec((MEM, DH * GROUP), lambda h: (1, h))


def both_spec():
    return pl.BlockSpec((2 * MEM, DH * GROUP), lambda h: (0, h))


def whole(*shape):
    return pl.BlockSpec(shape, lambda h: (0,) * len(shape))


TOKENS = jax.ShapeDtypeStruct((1, SEG, COLS), jnp.bfloat16)
COLUMNS = jax.ShapeDtypeStruct((SEG, COLS), jnp.float32)
COLUMNS_B = jax.ShapeDtypeStruct((SEG, COLS), jnp.bfloat16)
SQUARES = jax.ShapeDtypeStruct((HEADS, SEG, SEG), jnp.float32)
SQUARES_B = jax.ShapeDtypeStruct((HEADS, SEG, SEG), jnp.bfloat16)


def call(kernel, in_specs, outs, scratch=()):
    return pl.pallas_call(
        kernel,
        grid=(STEPS,),
        in_specs=in_specs,
        out_shape=tuple(shape for shape, _ in outs),
        out_specs=tuple(spec for _, spec in outs),
        scratch_shapes=[pltpu.VMEM(shape, jnp.float32) for shape in scratch],
        compiler_params=pltpu.CompilerParams(vmem_limit_bytes=48 << 20),
        name=kernel.__name__,
    )


def segment(kept, q, ks, vs, bias):
    return call(
        segment_kernel,
        [pl.BlockSpec(memory_space=pltpu.SMEM)] + [token_spec()] * 3 + [whole(HEADS, POS)],
        [
            (SQUARES_B, square_spec()),
            (COLUMNS, column_spec()),
            (COLUMNS, column_spec()),
            (COLUMNS, column_spec()),
            (SQUARES, square_spec()),
        ],
    )(kept, q, ks, vs, bias)


def forward(q, mem, mem_bias, cot, gain, seg_out, seg_top, seg_total):
    return call(
        forward_kernel,
        [token_spec(), both_spec(), square_spec(), token_spec(), gain_spec()]
        + [column_spec()] * 3,
        [
            (COLUMNS, column_spec()),
            (SQUARES_B, square_spec()),
            (COLUMNS, column_spec()),
            (COLUMNS, column_spec()),
            (jax.ShapeDtypeStruct((8, SEG), jnp.float32), whole(8, SEG)),
        ],
        [(SEG, DH), (SEG, DH)],
    )(q, mem, mem_bias, cot, gain, seg_out, seg_top, seg_total)


def score_grad(stats, vs, mem, cot, gain, attn, prob_mem, prob_seg, factor_mem, factor_seg):
    return call(
        score_grad_kernel,
        [whole(8, SEG)] * 4
        + [token_spec(), values_spec(), token_spec(), gain_spec(), column_spec()]
        + [square_spec()] * 2
        + [column_spec()] * 2,
        [
            (SQUARES_B, square_spec()),
            (SQUARES_B, square_spec()),
            (COLUMNS_B, column_spec()),
            (TOKENS, token_spec()),
            (jax.ShapeDtypeStruct((DP, 8, DH), jnp.bfloat16), whole(DP, 8, DH)),
        ],
        [(SEG, DH), (SEG, DH), (8, DH), (8, POS)],
    )(*stats, vs, mem, cot, gain, attn, prob_mem, prob_seg, factor_mem, factor_seg)


def input_grad(q, ks, mem, ds_mem, ds_seg, prob_seg, og_seg):
    return call(
        input_grad_kernel,
        [token_spec(), token_spec(), keys_spec()] + [square_spec()] * 3 + [column_spec()],
        [(TOKENS, token_spec())] * 3,
    )(q, ks, mem, ds_mem, ds_seg, prob_seg, og_seg)


def collect_kernel(share_ref, bias_ref, gain_ref):
    total = jnp.sum(share_ref[...].astype(jnp.float32), axis=0)
    gain_ref[...] = total[:HEADS]
    bias = stagger(jnp.broadcast_to(total[HEADS : HEADS + 1], (8, DH)), -8)
    bias_ref[...] = bias[:HEADS, :8]


def collect(shares):
    return pl.pallas_call(
        collect_kernel,
        out_shape=(
            jax.ShapeDtypeStruct((HEADS, 8), jnp.float32),
            jax.ShapeDtypeStruct((HEADS, DH), jnp.float32),
        ),
        name="collect",
    )(shares)


def exchange(x):
    return lax.all_to_all(x, "dp", split_axis=0, concat_axis=0, tiled=True)


def body(
    seg_queries, seg_keys, seg_values, memory_keys, memory_values,
    new_owner, kept_blocks, rel_bias, norm_gain, cotangent,
):
    own_index = lax.axis_index("dp")
    kept = jnp.sum(jnp.where(new_owner == own_index, kept_blocks, 0)).reshape(1)
    gain = norm_gain.reshape(1, COLS)
    pieces = jnp.concatenate([memory_keys[0], memory_values[0]], axis=0)
    spread = exchange(pieces.reshape(DP, PIECE, COLS))
    mem = exchange(reorder(new_owner, spread)).reshape(2 * MEM, COLS)
    prob_seg, seg_out, seg_top, seg_total, mem_bias = segment(
        kept, seg_queries, seg_keys, seg_values, rel_bias
    )
    attn, prob_mem, factor_mem, factor_seg, stats = forward(
        seg_queries, mem, mem_bias, cotangent, gain, seg_out, seg_top, seg_total
    )
    others = [
        lax.ppermute(stats, "mp", [(i, (i + step) % 4) for i in range(4)]) for step in (1, 2, 3)
    ]
    ds_mem, ds_seg, og_seg, attended, shares = score_grad(
        [stats] + others, seg_values, mem, cotangent, gain, attn,
        prob_mem, prob_seg, factor_mem, factor_seg,
    )
    query_grad, key_grad, value_grad = input_grad(
        seg_queries, seg_keys, mem, ds_mem, ds_seg, prob_seg, og_seg
    )
    bias_grad, gain_grad = collect(exchange(shares))
    return attended, query_grad, key_grad, value_grad, bias_grad, gain_grad.reshape(COLS)


def solution(mesh):
    row = P("dp", None, "mp")
    return jax.shard_map(
        body,
        mesh=mesh,
        in_specs=(row, row, row, row, row, P(), P(), P("mp", None), P("mp"), row),
        out_specs=(row, row, row, row, P("mp", "dp"), P("mp")),
        check_vma=False,
    )
```

```python
import math

import jax
import jax.numpy as jnp
from jax import lax
from jax.experimental import pallas as pl
from jax.experimental.pallas import tpu as pltpu
from jax.sharding import PartitionSpec as P

DH = 128
BLOCK = 128
HD = 3072
SEG = 256
MEM = 256
POS = 512
HEADS = 6
COLS = HEADS * DH
DP = 64
PIECE = (2 * MEM) // DP
LOG2E = math.log2(math.e)
SCALE = DH ** (-0.5)
FACTOR = SCALE * LOG2E
GROUP = 3
CHUNK = 16
LIMIT = 16
NT = (((1,), (1,)), ((), ()))
NN = (((1,), (0,)), ((), ()))
TN = (((0,), (0,)), ((), ()))


def dot(a, b, dims):
    return lax.dot_general(a, b, dims, preferred_element_type=jnp.float32)


def roll(x, shift):
    shift = shift % x.shape[1]
    return x if shift == 0 else pltpu.roll(x, shift, axis=1)


def reverse_lanes(x):
    rows, width = x.shape
    index = 127 - lax.broadcasted_iota(jnp.int32, (rows, 128), 1)
    parts = [
        jnp.take_along_axis(x[:, start : start + 128], index, axis=1)
        for start in range(width - 128, -1, -128)
    ]
    return jnp.concatenate(parts, axis=1)


def by_distance(x):
    return roll(reverse_lanes(x), -255)


def stagger(x, unit):
    row = lax.broadcasted_iota(jnp.int32, x.shape, 0)
    for bit in (1, 2, 4):
        x = jnp.where((row & bit) != 0, roll(x, bit * unit), x)
    return x


def bias_rows(table, head):
    base = stagger(jnp.broadcast_to(table[head : head + 1], (8, POS)), 1)
    return jnp.concatenate([roll(base, 8 * group) for group in range(SEG // 8)], axis=0)


def diagonal_row(score_grad):
    level = [score_grad[8 * g : 8 * g + 8] for g in range(SEG // 8)]
    while len(level) > 1:
        half = len(level) // 2
        level = [level[k] + roll(level[k + half], -8 * half) for k in range(half)]
    return jnp.sum(stagger(level[0], -1), axis=0, keepdims=True)


def reorder_kernel(owner_ref, in_ref, out_ref, held_ref, source_ref, sem):
    for slot in range(DP):
        source_ref[owner_ref[slot]] = slot
    copies = []
    for part in range(DP // CHUNK):
        for dest in range(CHUNK * part, CHUNK * part + CHUNK):
            held_ref[dest] = in_ref[source_ref[dest]]
        rows = pl.ds(CHUNK * part, CHUNK)
        copy = pltpu.make_async_copy(held_ref.at[rows], out_ref.at[rows], sem.at[part])
        copy.start()
        copies.append(copy)
    for copy in copies:
        copy.wait()


def reorder(new_owner, pieces):
    return pl.pallas_call(
        reorder_kernel,
        out_shape=pltpu.HBM(pieces.shape, pieces.dtype),
        in_specs=[
            pl.BlockSpec(memory_space=pltpu.SMEM),
            pl.BlockSpec(memory_space=pltpu.VMEM),
        ],
        out_specs=pl.BlockSpec(memory_space=pl.ANY),
        scratch_shapes=[
            pltpu.VMEM(pieces.shape, pieces.dtype),
            pltpu.SMEM((DP,), jnp.int32),
            pltpu.SemaphoreType.DMA((DP // CHUNK,)),
        ],
        name="reorder",
    )(new_owner, near(pieces))


def segment_kernel(
    kept_ref, q_ref, ks_ref, vs_ref, bias_ref, prob_ref, out_ref, row_ref, mem_bias_ref
):
    col = lax.broadcasted_iota(jnp.int32, (SEG, SEG), 1)
    row = lax.broadcasted_iota(jnp.int32, (SEG, SEG), 0)
    lane = lax.broadcasted_iota(jnp.int32, (SEG, DH), 1)
    rows = jnp.zeros((SEG, DH), jnp.float32)
    ones = jnp.ones((SEG, DH), jnp.bfloat16)
    seen = col >= MEM - BLOCK * kept_ref[0]
    table = by_distance(bias_ref[...] * LOG2E)
    for g in range(HEADS):
        cols = slice(DH * g, DH * g + DH)
        bias = bias_rows(table, g)
        mem_bias_ref[g] = jnp.where(seen, bias[:, :MEM], -1e30)
        scores = dot(q_ref[0, :, cols], ks_ref[0, :, cols], NT) * FACTOR
        scores = jnp.where(col <= row, scores + bias[:, MEM:], -1e30)
        top = jnp.max(scores, axis=1, keepdims=True)
        prob = jnp.exp2(scores - top).astype(jnp.bfloat16)
        prob_ref[g] = prob
        both = dot(prob, jnp.concatenate([vs_ref[0, :, cols], ones], axis=1), NN)
        out_ref[g] = both[:, :DH]
        rows = jnp.where(lane == g, top, jnp.where(lane == 8 + g, both[:, DH:], rows))
    row_ref[...] = rows


def forward_kernel(
    q_ref, mem_ref, gain_ref, mem_bias_ref, seg_row_ref, seg_out_hbm, cot_hbm,
    out_ref, prob_ref, factor_mem_ref, factor_seg_ref, stats_ref,
    seg_out_ref, cot_ref, sem,
):
    copies = (
        pltpu.make_async_copy(seg_out_hbm, seg_out_ref, sem.at[0]),
        pltpu.make_async_copy(cot_hbm.at[0], cot_ref, sem.at[1]),
    )
    for copy in copies:
        copy.start()
    ones = jnp.ones((MEM, DH), jnp.bfloat16)
    seg_row = seg_row_ref[...]
    for g in range(HEADS):
        cols = slice(DH * g, DH * g + DH)
        scores = dot(q_ref[0, :, cols], mem_ref[:MEM, cols], NT) * FACTOR + mem_bias_ref[g]
        seg_top = jnp.broadcast_to(seg_row[:, g : g + 1], (SEG, DH))
        seg_total = jnp.broadcast_to(seg_row[:, 8 + g : 9 + g], (SEG, DH))
        top = jnp.maximum(jnp.max(scores, axis=1, keepdims=True), seg_top)
        prob = jnp.exp2(scores - jnp.concatenate([top, top], axis=1)).astype(jnp.bfloat16)
        prob_ref[g] = prob
        both = dot(prob, jnp.concatenate([mem_ref[MEM:, cols], ones], axis=1), NN)
        shrink = jnp.exp2(seg_top - top)
        inverse = 1.0 / (both[:, DH:] + seg_total * shrink)
        factor_mem_ref[:, cols] = inverse
        factor_seg_ref[:, cols] = shrink * inverse
        out_ref[:, cols] = both[:, :DH] * inverse
    for copy in copies:
        copy.wait()
    square = cross = None
    for g in range(HEADS):
        cols = slice(DH * g, DH * g + DH)
        out = out_ref[:, cols] + seg_out_ref[g] * factor_seg_ref[:, cols]
        out_ref[:, cols] = out
        part = cot_ref[:, cols].astype(jnp.float32) * gain_ref[:, cols] * out
        square = out * out if g == 0 else square + out * out
        cross = part if g == 0 else cross + part
    stats_ref[...] = jnp.zeros((8, SEG), jnp.float32)
    stats_ref[0:1, :] = jnp.sum(square.T, axis=0, keepdims=True)
    stats_ref[1:2, :] = jnp.sum(cross.T, axis=0, keepdims=True)


def score_grad_kernel(
    stats0_ref, stats1_ref, stats2_ref, stats3_ref,
    vs_ref, mem_ref, cot_ref, gain_ref, attn_ref, prob_mem_ref, prob_seg_ref,
    factor_mem_ref, factor_seg_ref,
    attended_hbm, ds_mem_ref, ds_seg_ref, og_seg_ref, share_ref,
    attended_ref, sem,
):
    stats = (stats0_ref[...] + stats1_ref[...]) + (stats2_ref[...] + stats3_ref[...])
    inv = lax.rsqrt(stats[0:1] / HD + 1e-06)
    coef = inv * inv * inv * stats[1:2] / HD
    inv = jnp.broadcast_to(inv, (DH, SEG)).T
    coef = jnp.broadcast_to(coef, (DH, SEG)).T
    for g in range(HEADS):
        cols = slice(DH * g, DH * g + DH)
        attended_ref[:, cols] = (attn_ref[:, cols] * inv * gain_ref[:, cols]).astype(jnp.bfloat16)
    copy = pltpu.make_async_copy(attended_ref, attended_hbm.at[0], sem)
    copy.start()
    gains = []
    diagonals = []
    for g in range(HEADS):
        cols = slice(DH * g, DH * g + DH)
        attn = attn_ref[:, cols]
        gain = gain_ref[:, cols]
        upstream = cot_ref[0, :, cols].astype(jnp.float32)
        normed = attn * inv
        gains.append(jnp.sum(upstream * normed, axis=0, keepdims=True))
        out_grad = inv * (upstream * gain) - attn * coef
        delta = jnp.sum(out_grad * attn, axis=1, keepdims=True)
        factor_mem = factor_mem_ref[:, cols]
        factor_seg = factor_seg_ref[:, cols]
        og_mem = (out_grad * factor_mem).astype(jnp.bfloat16)
        og_seg = (out_grad * factor_seg).astype(jnp.bfloat16)
        og_seg_ref[g] = og_seg
        less_mem = delta * factor_mem
        less_seg = delta * factor_seg
        dp_mem = dot(og_mem, mem_ref[MEM:, cols], NT) - jnp.concatenate([less_mem, less_mem], axis=1)
        dp_seg = dot(og_seg, vs_ref[0, :, cols], NT) - jnp.concatenate([less_seg, less_seg], axis=1)
        ds_mem = prob_mem_ref[g].astype(jnp.float32) * dp_mem
        ds_seg = prob_seg_ref[g].astype(jnp.float32) * dp_seg
        ds_mem_ref[g] = ds_mem.astype(jnp.bfloat16)
        ds_seg_ref[g] = ds_seg.astype(jnp.bfloat16)
        diagonals.append(diagonal_row(jnp.concatenate([ds_mem, ds_seg], axis=1)))

    pad = [jnp.zeros((2, DH), jnp.float32)]
    gains = jnp.concatenate(gains + pad, axis=0)
    diagonals = jnp.concatenate(diagonals + [jnp.zeros((2, POS), jnp.float32)], axis=0)
    bias = stagger(by_distance(diagonals), 8)
    bias = jnp.concatenate([bias, bias[:, :128]], axis=1)
    lane = lax.broadcasted_iota(jnp.int32, (8, DH), 1)
    row = lax.broadcasted_iota(jnp.int32, (8, DH), 0)
    own = (lane >= 8 * row) & (lane < 8 * row + 8) & (row < HEADS)
    for dest in range(DP):
        start, shift = divmod(8 * dest, 128)
        here = bias[:, 128 * start : 128 * start + 128]
        after = bias[:, 128 * start + 128 : 128 * start + 256]
        part = jnp.where(lane < 128 - shift, roll(here, -shift), roll(after, -shift))
        part = jnp.sum(jnp.where(own, part, 0.0), axis=0, keepdims=True)
        share_ref[dest] = jnp.where(row == HEADS, part, gains).astype(share_ref.dtype)
    copy.wait()


def input_grad_kernel(
    q_ref, ks_ref, mem_ref, ds_mem_ref, ds_seg_ref, prob_seg_ref, og_seg_ref,
    dq_ref, dk_ref, dv_ref,
):
    for g in range(GROUP):
        cols = slice(DH * g, DH * g + DH)
        ds_seg = ds_seg_ref[g]
        dq = dot(ds_mem_ref[g], mem_ref[:, cols], NN) + dot(ds_seg, ks_ref[0, :, cols], NN)
        dq_ref[0, :, cols] = (dq * SCALE).astype(jnp.bfloat16)
        dk_ref[0, :, cols] = (dot(ds_seg, q_ref[0, :, cols], TN) * SCALE).astype(jnp.bfloat16)
        dv_ref[0, :, cols] = dot(prob_seg_ref[g], og_seg_ref[g], TN).astype(jnp.bfloat16)


TOKENS = jax.ShapeDtypeStruct((1, SEG, COLS), jnp.bfloat16)
COLUMNS = jax.ShapeDtypeStruct((SEG, COLS), jnp.float32)
HEAD_COLUMNS = jax.ShapeDtypeStruct((HEADS, SEG, DH), jnp.float32)
HEAD_COLUMNS_B = jax.ShapeDtypeStruct((HEADS, SEG, DH), jnp.bfloat16)
ROWS = jax.ShapeDtypeStruct((SEG, DH), jnp.float32)
STATS = jax.ShapeDtypeStruct((8, SEG), jnp.float32)
SHARES = jax.ShapeDtypeStruct((DP, 8, DH), jnp.bfloat16)
SQUARES = jax.ShapeDtypeStruct((HEADS, SEG, SEG), jnp.float32)
SQUARES_B = jax.ShapeDtypeStruct((HEADS, SEG, SEG), jnp.bfloat16)


def far(x):
    return pltpu.with_memory_space_constraint(x, pltpu.HBM)


def far_out(shape):
    return pltpu.HBM(shape.shape, shape.dtype)


def near(x):
    return pltpu.with_memory_space_constraint(x, pltpu.VMEM)


def near_out(shape):
    return pltpu.VMEM(shape.shape, shape.dtype)


def near_call(kernel, scalars, ins, far_ins, outs, far_outs, tail=(), scratch=()):
    spec = pl.BlockSpec(memory_space=pltpu.VMEM)
    any_spec = pl.BlockSpec(memory_space=pl.ANY)
    return pl.pallas_call(
        kernel,
        in_specs=[pl.BlockSpec(memory_space=pltpu.SMEM)] * len(scalars)
        + [spec] * len(ins)
        + [any_spec] * len(far_ins),
        out_shape=tuple(far_out(x) for x in far_outs) + tuple(outs) + tuple(tail),
        out_specs=(any_spec,) * len(far_outs) + (spec,) * (len(outs) + len(tail)),
        scratch_shapes=scratch,
        compiler_params=pltpu.CompilerParams(vmem_limit_bytes=LIMIT << 20),
        name=kernel.__name__,
    )(*scalars, *[near(x) for x in ins], *[far(x) for x in far_ins])


def segment(kept, q, ks, vs, bias):
    return near_call(
        segment_kernel, (kept,), (q, ks, vs, bias), (),
        [far_out(SQUARES_B), far_out(HEAD_COLUMNS), near_out(ROWS), near_out(SQUARES)], (),
    )


def forward(q, mem, gain, mem_bias, seg_row, seg_out, cot):
    return near_call(
        forward_kernel,
        (),
        (q, mem, gain, mem_bias, seg_row),
        (seg_out, cot),
        [near_out(x) for x in (COLUMNS, SQUARES_B, COLUMNS, COLUMNS, STATS)],
        (),
        scratch=[
            pltpu.VMEM((HEADS, SEG, DH), jnp.float32),
            pltpu.VMEM((SEG, COLS), jnp.bfloat16),
            pltpu.SemaphoreType.DMA((2,)),
        ],
    )


def score_grad(stats, vs, mem, cot, gain, attn, prob_mem, prob_seg, factor_mem, factor_seg):
    return near_call(
        score_grad_kernel,
        (),
        (*stats, vs, mem, cot, gain, attn, prob_mem, prob_seg, factor_mem, factor_seg),
        (),
        [near_out(x) for x in (SQUARES_B, SQUARES_B, HEAD_COLUMNS_B)] + [far_out(SHARES)],
        (TOKENS,),
        scratch=[
            pltpu.VMEM((SEG, COLS), jnp.bfloat16),
            pltpu.SemaphoreType.DMA,
        ],
    )


def input_grad(q, ks, mem, ds_mem, ds_seg, prob_seg, og_seg):
    tokens = pl.BlockSpec((1, SEG, DH * GROUP), lambda h: (0, 0, h))
    squares = pl.BlockSpec((GROUP, SEG, SEG), lambda h: (h, 0, 0))
    return pl.pallas_call(
        input_grad_kernel,
        grid=(HEADS // GROUP,),
        in_specs=[
            tokens,
            tokens,
            pl.BlockSpec((MEM, DH * GROUP), lambda h: (0, h)),
            squares,
            squares,
            squares,
            pl.BlockSpec((GROUP, SEG, DH), lambda h: (h, 0, 0)),
        ],
        out_shape=tuple(far_out(TOKENS) for _ in range(3)),
        out_specs=(tokens,) * 3,
        compiler_params=pltpu.CompilerParams(vmem_limit_bytes=LIMIT << 20),
        name="input_grad_kernel",
    )(far(q), far(ks), near(mem), near(ds_mem), near(ds_seg), far(prob_seg), near(og_seg))


def collect_kernel(share_ref, bias_ref, gain_ref):
    total = jnp.sum(share_ref[...].astype(jnp.float32), axis=0)
    gain_ref[...] = total[:HEADS]
    bias = stagger(jnp.broadcast_to(total[HEADS : HEADS + 1], (8, DH)), -8)
    bias_ref[...] = bias[:HEADS, :8]


def collect(shares):
    return pl.pallas_call(
        collect_kernel,
        in_specs=[pl.BlockSpec(memory_space=pltpu.VMEM)],
        out_shape=(
            pltpu.HBM((HEADS, 8), jnp.float32),
            pltpu.HBM((HEADS, DH), jnp.float32),
        ),
        name="collect",
    )(near(shares))


def exchange(x):
    return lax.all_to_all(x, "dp", split_axis=0, concat_axis=0, tiled=True)


def body(
    seg_queries, seg_keys, seg_values, memory_keys, memory_values,
    new_owner, kept_blocks, rel_bias, norm_gain, cotangent,
):
    own_index = lax.axis_index("dp")
    kept = jnp.sum(jnp.where(new_owner == own_index, kept_blocks, 0)).reshape(1)
    gain = norm_gain.reshape(1, COLS)
    pieces = jnp.concatenate([memory_keys[0], memory_values[0]], axis=0)
    spread = exchange(pieces.reshape(DP, PIECE, COLS))
    mem = exchange(reorder(new_owner, spread)).reshape(2 * MEM, COLS)
    bias = jnp.pad(rel_bias, ((0, 8 - HEADS), (0, 0)))
    prob_seg, seg_out, seg_row, mem_bias = segment(
        kept, seg_queries, seg_keys, seg_values, bias
    )
    attn, prob_mem, factor_mem, factor_seg, stats = forward(
        seg_queries, mem, gain, mem_bias, seg_row, seg_out, cotangent
    )
    others = [
        lax.ppermute(stats, "mp", [(i, (i + step) % 4) for i in range(4)]) for step in (1, 2, 3)
    ]
    attended, ds_mem, ds_seg, og_seg, shares = score_grad(
        [stats] + others, seg_values, mem, cotangent, gain, attn,
        prob_mem, prob_seg, factor_mem, factor_seg,
    )
    query_grad, key_grad, value_grad = input_grad(
        seg_queries, seg_keys, mem, ds_mem, ds_seg, prob_seg, og_seg
    )
    bias_grad, gain_grad = collect(exchange(shares))
    return attended, query_grad, key_grad, value_grad, bias_grad, gain_grad.reshape(COLS)


def solution(mesh):
    row = P("dp", None, "mp")
    return jax.shard_map(
        body,
        mesh=mesh,
        in_specs=(row, row, row, row, row, P(), P(), P("mp", None), P("mp"), row),
        out_specs=(row, row, row, row, P("mp", "dp"), P("mp")),
        check_vma=False,
    )
```

```python
import math

import jax
import jax.numpy as jnp
from jax import lax
from jax.experimental import pallas as pl
from jax.experimental.pallas import tpu as pltpu
from jax.sharding import PartitionSpec as P

DH = 128
BLOCK = 128
HD = 3072
SEG = 256
HALF = SEG // 2
MEM = 256
POS = 512
HEADS = 6
COLS = HEADS * DH
DP = 64
PIECE = (2 * MEM) // DP
LOG2E = math.log2(math.e)
SCALE = DH ** (-0.5)
FACTOR = SCALE * LOG2E
GROUP = 3
CHUNK = 16
LIMIT = 16
NT = (((1,), (1,)), ((), ()))
NN = (((1,), (0,)), ((), ()))
TN = (((0,), (0,)), ((), ()))


def dot(a, b, dims):
    return lax.dot_general(a, b, dims, preferred_element_type=jnp.float32)


def roll(x, shift):
    shift = shift % x.shape[1]
    return x if shift == 0 else pltpu.roll(x, shift, axis=1)


def reverse_lanes(x):
    rows, width = x.shape
    index = 127 - lax.broadcasted_iota(jnp.int32, (rows, 128), 1)
    parts = [
        jnp.take_along_axis(x[:, start : start + 128], index, axis=1)
        for start in range(width - 128, -1, -128)
    ]
    return jnp.concatenate(parts, axis=1)


def by_distance(x):
    return roll(reverse_lanes(x), -255)


def stagger(x, unit):
    row = lax.broadcasted_iota(jnp.int32, x.shape, 0)
    for bit in (1, 2, 4):
        x = jnp.where((row & bit) != 0, roll(x, bit * unit), x)
    return x


def bias_rows(table, head):
    base = stagger(jnp.broadcast_to(table[head : head + 1], (8, POS)), 1)
    return jnp.concatenate([roll(base, 8 * group) for group in range(SEG // 8)], axis=0)


def diagonal_row(score_grad):
    level = [score_grad[8 * g : 8 * g + 8] for g in range(SEG // 8)]
    while len(level) > 1:
        half = len(level) // 2
        level = [level[k] + roll(level[k + half], -8 * half) for k in range(half)]
    return jnp.sum(stagger(level[0], -1), axis=0, keepdims=True)


def reorder_kernel(owner_ref, in_ref, out_ref, held_ref, source_ref, sem):
    for slot in range(DP):
        source_ref[owner_ref[slot]] = slot
    copies = []
    for part in range(DP // CHUNK):
        for dest in range(CHUNK * part, CHUNK * part + CHUNK):
            held_ref[dest] = in_ref[source_ref[dest]]
        rows = pl.ds(CHUNK * part, CHUNK)
        copy = pltpu.make_async_copy(held_ref.at[rows], out_ref.at[rows], sem.at[part])
        copy.start()
        copies.append(copy)
    for copy in copies:
        copy.wait()


def reorder(new_owner, pieces):
    return pl.pallas_call(
        reorder_kernel,
        out_shape=pltpu.HBM(pieces.shape, pieces.dtype),
        in_specs=[
            pl.BlockSpec(memory_space=pltpu.SMEM),
            pl.BlockSpec(memory_space=pltpu.VMEM),
        ],
        out_specs=pl.BlockSpec(memory_space=pl.ANY),
        scratch_shapes=[
            pltpu.VMEM(pieces.shape, pieces.dtype),
            pltpu.SMEM((DP,), jnp.int32),
            pltpu.SemaphoreType.DMA((DP // CHUNK,)),
        ],
        name="reorder",
    )(new_owner, near(pieces))


def segment_kernel(
    q_ref, ks_ref, vs_ref, bias_ref, gain_ref, prob_ref, out_ref, table_ref
):
    col = lax.broadcasted_iota(jnp.int32, (SEG, SEG), 1)
    row = lax.broadcasted_iota(jnp.int32, (SEG, SEG), 0)
    lane = lax.broadcasted_iota(jnp.int32, (SEG, DH), 1)
    rows = jnp.zeros((SEG, DH), jnp.float32)
    ones = jnp.ones((SEG, DH), jnp.bfloat16)
    table = by_distance(bias_ref[...] * LOG2E)
    for g in range(HEADS):
        cols = slice(DH * g, DH * g + DH)
        bias = bias_rows(table, g)
        table_ref[HALF * g : HALF * g + HALF] = jnp.concatenate(
            [bias[HALF:, :DH], bias[:HALF, :MEM]], axis=1
        )
        scores = dot(q_ref[0, :, cols], ks_ref[0, :, cols], NT) * FACTOR
        scores = jnp.where(col <= row, scores + bias[:, MEM:], -1e30)
        top = jnp.max(scores, axis=1, keepdims=True)
        prob = jnp.exp2(scores - top).astype(jnp.bfloat16)
        prob_ref[g] = prob
        both = dot(prob, jnp.concatenate([vs_ref[0, :, cols], ones], axis=1), NN)
        out_ref[g] = both[:, :DH]
        rows = jnp.where(lane == g, top, jnp.where(lane == 8 + g, both[:, DH:], rows))
    table_ref[HALF * HEADS : HALF * HEADS + 16, :SEG] = rows.T[:16]
    for g in range(0, HEADS, 3):
        row = HALF * HEADS + 16 + g // 3
        table_ref[row : row + 1] = gain_ref[:, DH * g : DH * g + 3 * DH]


def forward_kernel(
    kept_ref, q_ref, mem_ref, table_ref, seg_out_hbm, cot_hbm,
    out_ref, prob_ref, factor_mem_ref, factor_seg_ref, stats_ref,
    seg_out_ref, cot_ref, sem,
):
    copies = (
        pltpu.make_async_copy(seg_out_hbm, seg_out_ref, sem.at[0]),
        pltpu.make_async_copy(cot_hbm.at[0], cot_ref, sem.at[1]),
    )
    for copy in copies:
        copy.start()
    ones = jnp.ones((MEM, DH), jnp.bfloat16)
    seg_row = table_ref[HALF * HEADS : HALF * HEADS + 16, :SEG]
    both_kept = jnp.full((SEG, BLOCK), kept_ref[0], jnp.int32) > 1
    for g in range(HEADS):
        cols = slice(DH * g, DH * g + DH)
        scores = dot(q_ref[0, :, cols], mem_ref[:MEM, cols], NT) * FACTOR
        bias = table_ref[HALF * g : HALF * g + HALF]
        scores = scores + jnp.concatenate([bias[:, DH:], bias[:, :MEM]], axis=0)
        scores = jnp.concatenate([jnp.where(both_kept, scores[:, :BLOCK], -1e30), scores[:, BLOCK:]], axis=1)
        seg_top = jnp.broadcast_to(seg_row[g : g + 1], (DH, SEG)).T
        seg_total = jnp.broadcast_to(seg_row[8 + g : 9 + g], (DH, SEG)).T
        top = jnp.maximum(jnp.max(scores, axis=1, keepdims=True), seg_top)
        prob = jnp.exp2(scores - jnp.concatenate([top, top], axis=1)).astype(jnp.bfloat16)
        prob_ref[g] = prob
        both = dot(prob, jnp.concatenate([mem_ref[MEM:, cols], ones], axis=1), NN)
        shrink = jnp.exp2(seg_top - top)
        inverse = 1.0 / (both[:, DH:] + seg_total * shrink)
        factor_mem_ref[:, cols] = inverse
        factor_seg_ref[:, cols] = shrink * inverse
        out_ref[:, cols] = both[:, :DH] * inverse
    for copy in copies:
        copy.wait()
    square = cross = None
    for g in range(HEADS):
        cols = slice(DH * g, DH * g + DH)
        out = out_ref[:, cols] + seg_out_ref[g] * factor_seg_ref[:, cols]
        out_ref[:, cols] = out
        row = HALF * HEADS + 16 + g // 3
        gain = table_ref[row : row + 1, DH * (g % 3) : DH * (g % 3) + DH]
        part = cot_ref[:, cols].astype(jnp.float32) * gain * out
        square = out * out if g == 0 else square + out * out
        cross = part if g == 0 else cross + part
    stats_ref[...] = jnp.zeros((8, SEG), jnp.float32)
    stats_ref[0:1, :] = jnp.sum(square.T, axis=0, keepdims=True)
    stats_ref[1:2, :] = jnp.sum(cross.T, axis=0, keepdims=True)


def score_grad_kernel(
    stats0_ref, stats1_ref, stats2_ref, stats3_ref,
    mem_ref, cot_ref, gain_ref, attn_ref, prob_mem_ref, prob_seg_ref,
    factor_mem_ref, factor_seg_ref, vs_hbm,
    attended_hbm, og_seg_hbm, keys_hbm, ds_mem_ref, ds_seg_ref, share_ref,
    attended_ref, og_seg_ref, og_mem_ref, less_ref, vs_ref, sem,
):
    values_copy = pltpu.make_async_copy(vs_hbm.at[0], vs_ref, sem.at[0])
    values_copy.start()
    keys_copy = pltpu.make_async_copy(mem_ref.at[pl.ds(0, MEM)], keys_hbm, sem.at[1])
    keys_copy.start()
    stats = (stats0_ref[...] + stats1_ref[...]) + (stats2_ref[...] + stats3_ref[...])
    inv = lax.rsqrt(stats[0:1] / HD + 1e-06)
    coef = inv * inv * inv * stats[1:2] / HD
    inv = jnp.broadcast_to(inv, (DH, SEG)).T
    coef = jnp.broadcast_to(coef, (DH, SEG)).T
    gains = []
    for g in range(HEADS):
        cols = slice(DH * g, DH * g + DH)
        attn = attn_ref[:, cols]
        gain = gain_ref[:, cols]
        upstream = cot_ref[0, :, cols].astype(jnp.float32)
        normed = attn * inv
        attended_ref[:, cols] = (normed * gain).astype(jnp.bfloat16)
        gains.append(jnp.sum(upstream * normed, axis=0, keepdims=True))
        out_grad = inv * (upstream * gain) - attn * coef
        less_ref[g] = jnp.broadcast_to(
            jnp.sum(out_grad * attn, axis=1, keepdims=True), (SEG, DH)
        )
        og_mem_ref[g] = (out_grad * factor_mem_ref[:, cols]).astype(jnp.bfloat16)
        og_seg_ref[g] = (out_grad * factor_seg_ref[:, cols]).astype(jnp.bfloat16)
    copies = (
        pltpu.make_async_copy(attended_ref, attended_hbm.at[0], sem.at[2]),
        pltpu.make_async_copy(og_seg_ref, og_seg_hbm, sem.at[3]),
    )
    for copy in copies:
        copy.start()
    values_copy.wait()
    diagonals = []
    for g in range(HEADS):
        cols = slice(DH * g, DH * g + DH)
        less_mem = less_ref[g] * factor_mem_ref[:, cols]
        less_seg = less_ref[g] * factor_seg_ref[:, cols]
        dp_mem = dot(og_mem_ref[g], mem_ref[MEM:, cols], NT)
        dp_seg = dot(og_seg_ref[g], vs_ref[:, cols], NT)
        dp_mem = dp_mem - jnp.concatenate([less_mem, less_mem], axis=1)
        dp_seg = dp_seg - jnp.concatenate([less_seg, less_seg], axis=1)
        ds_mem = prob_mem_ref[g].astype(jnp.float32) * dp_mem
        ds_seg = prob_seg_ref[g].astype(jnp.float32) * dp_seg
        ds_mem_ref[g] = ds_mem.astype(jnp.bfloat16)
        ds_seg_ref[g] = ds_seg.astype(jnp.bfloat16)
        diagonals.append(diagonal_row(jnp.concatenate([ds_mem, ds_seg], axis=1)))

    pad = [jnp.zeros((2, DH), jnp.float32)]
    gains = jnp.concatenate(gains + pad, axis=0)
    diagonals = jnp.concatenate(diagonals + [jnp.zeros((2, POS), jnp.float32)], axis=0)
    bias = stagger(by_distance(diagonals), 8)
    bias = jnp.concatenate([bias, bias[:, :128]], axis=1)
    lane = lax.broadcasted_iota(jnp.int32, (8, DH), 1)
    row = lax.broadcasted_iota(jnp.int32, (8, DH), 0)
    own = (lane >= 8 * row) & (lane < 8 * row + 8) & (row < HEADS)
    for dest in range(DP):
        start, shift = divmod(8 * dest, 128)
        here = bias[:, 128 * start : 128 * start + 128]
        after = bias[:, 128 * start + 128 : 128 * start + 256]
        part = jnp.where(lane < 128 - shift, roll(here, -shift), roll(after, -shift))
        part = jnp.sum(jnp.where(own, part, 0.0), axis=0, keepdims=True)
        share_ref[dest] = jnp.where(row == HEADS, part, gains).astype(share_ref.dtype)
    keys_copy.wait()
    for copy in copies:
        copy.wait()


def input_grad_kernel(
    q_ref, ks_ref, mem_ref, ds_mem_ref, ds_seg_ref, prob_seg_ref, og_seg_ref,
    dq_ref, dk_ref, dv_ref,
):
    for g in range(GROUP):
        cols = slice(DH * g, DH * g + DH)
        ds_seg = ds_seg_ref[g]
        dq = dot(ds_mem_ref[g], mem_ref[:, cols], NN) + dot(ds_seg, ks_ref[0, :, cols], NN)
        dq_ref[0, :, cols] = (dq * SCALE).astype(jnp.bfloat16)
        dk_ref[0, :, cols] = (dot(ds_seg, q_ref[0, :, cols], TN) * SCALE).astype(jnp.bfloat16)
        dv_ref[0, :, cols] = dot(prob_seg_ref[g], og_seg_ref[g], TN).astype(jnp.bfloat16)


TOKENS = jax.ShapeDtypeStruct((1, SEG, COLS), jnp.bfloat16)
COLUMNS = jax.ShapeDtypeStruct((SEG, COLS), jnp.float32)
HEAD_COLUMNS = jax.ShapeDtypeStruct((HEADS, SEG, DH), jnp.float32)
HEAD_COLUMNS_B = jax.ShapeDtypeStruct((HEADS, SEG, DH), jnp.bfloat16)
TABLE = jax.ShapeDtypeStruct((HEADS * HALF + 24, MEM + DH), jnp.float32)
STATS = jax.ShapeDtypeStruct((8, SEG), jnp.float32)
KEYS = jax.ShapeDtypeStruct((MEM, COLS), jnp.bfloat16)
SHARES = jax.ShapeDtypeStruct((DP, 8, DH), jnp.bfloat16)
SQUARES_B = jax.ShapeDtypeStruct((HEADS, SEG, SEG), jnp.bfloat16)


def far(x):
    return pltpu.with_memory_space_constraint(x, pltpu.HBM)


def far_out(shape):
    return pltpu.HBM(shape.shape, shape.dtype)


def near(x):
    return pltpu.with_memory_space_constraint(x, pltpu.VMEM)


def near_out(shape):
    return pltpu.VMEM(shape.shape, shape.dtype)


def near_call(kernel, scalars, ins, far_ins, outs, far_outs, tail=(), scratch=()):
    spec = pl.BlockSpec(memory_space=pltpu.VMEM)
    any_spec = pl.BlockSpec(memory_space=pl.ANY)
    return pl.pallas_call(
        kernel,
        in_specs=[pl.BlockSpec(memory_space=pltpu.SMEM)] * len(scalars)
        + [spec] * len(ins)
        + [any_spec] * len(far_ins),
        out_shape=tuple(far_out(x) for x in far_outs) + tuple(outs) + tuple(tail),
        out_specs=(any_spec,) * len(far_outs) + (spec,) * (len(outs) + len(tail)),
        scratch_shapes=scratch,
        compiler_params=pltpu.CompilerParams(vmem_limit_bytes=LIMIT << 20),
        name=kernel.__name__,
    )(*scalars, *[near(x) for x in ins], *[far(x) for x in far_ins])


def segment(q, ks, vs, bias, gain):
    spec = pl.BlockSpec(memory_space=pltpu.VMEM)
    return pl.pallas_call(
        segment_kernel,
        in_specs=[spec] * 5,
        out_shape=(
            far_out(SQUARES_B), far_out(HEAD_COLUMNS), near_out(TABLE),
        ),
        out_specs=(spec,) * 3,
        compiler_params=pltpu.CompilerParams(vmem_limit_bytes=LIMIT << 20),
        name="segment_kernel",
    )(far(q), far(ks), far(vs), bias, far(gain))


def forward(kept, q, mem, table, seg_out, cot):
    return near_call(
        forward_kernel,
        (kept,),
        (q, mem, table),
        (seg_out, cot),
        [near_out(x) for x in (COLUMNS, SQUARES_B, COLUMNS, COLUMNS, STATS)],
        (),
        scratch=[
            pltpu.VMEM((HEADS, SEG, DH), jnp.float32),
            pltpu.VMEM((SEG, COLS), jnp.bfloat16),
            pltpu.SemaphoreType.DMA((2,)),
        ],
    )


def score_grad(stats, vs, mem, cot, gain, attn, prob_mem, prob_seg, factor_mem, factor_seg):
    return near_call(
        score_grad_kernel,
        (),
        (*stats, mem, cot, gain, attn, prob_mem, prob_seg, factor_mem, factor_seg),
        (vs,),
        [near_out(SQUARES_B), near_out(SQUARES_B), far_out(SHARES)],
        (TOKENS, HEAD_COLUMNS_B, KEYS),
        scratch=[
            pltpu.VMEM((SEG, COLS), jnp.bfloat16),
            pltpu.VMEM((HEADS, SEG, DH), jnp.bfloat16),
            pltpu.VMEM((HEADS, SEG, DH), jnp.bfloat16),
            pltpu.VMEM((HEADS, SEG, DH), jnp.float32),
            pltpu.VMEM((SEG, COLS), jnp.bfloat16),
            pltpu.SemaphoreType.DMA((4,)),
        ],
    )


def input_grad(q, ks, keys, ds_mem, ds_seg, prob_seg, og_seg):
    tokens = pl.BlockSpec((1, SEG, DH * GROUP), lambda h: (0, 0, h))
    squares = pl.BlockSpec((GROUP, SEG, SEG), lambda h: (h, 0, 0))
    return pl.pallas_call(
        input_grad_kernel,
        grid=(HEADS // GROUP,),
        in_specs=[
            tokens,
            tokens,
            pl.BlockSpec((MEM, DH * GROUP), lambda h: (0, h)),
            squares,
            squares,
            squares,
            pl.BlockSpec((GROUP, SEG, DH), lambda h: (h, 0, 0)),
        ],
        out_shape=tuple(far_out(TOKENS) for _ in range(3)),
        out_specs=(tokens,) * 3,
        compiler_params=pltpu.CompilerParams(vmem_limit_bytes=LIMIT << 20),
        name="input_grad_kernel",
    )(far(q), far(ks), far(keys), near(ds_mem), near(ds_seg), far(prob_seg), far(og_seg))


def collect_kernel(share_ref, bias_ref, gain_ref):
    total = jnp.sum(share_ref[...].astype(jnp.float32), axis=0)
    gain_ref[...] = total[:HEADS]
    bias = stagger(jnp.broadcast_to(total[HEADS : HEADS + 1], (8, DH)), -8)
    bias_ref[...] = bias[:HEADS, :8]


def collect(shares):
    return pl.pallas_call(
        collect_kernel,
        in_specs=[pl.BlockSpec(memory_space=pltpu.VMEM)],
        out_shape=(
            pltpu.HBM((HEADS, 8), jnp.float32),
            pltpu.HBM((HEADS, DH), jnp.float32),
        ),
        name="collect",
    )(near(shares))


def exchange(x):
    return lax.all_to_all(x, "dp", split_axis=0, concat_axis=0, tiled=True)


def body(
    seg_queries, seg_keys, seg_values, memory_keys, memory_values,
    new_owner, kept_blocks, rel_bias, norm_gain, cotangent,
):
    own_index = lax.axis_index("dp")
    kept = jnp.sum(jnp.where(new_owner == own_index, kept_blocks, 0)).reshape(1)
    gain = norm_gain.reshape(1, COLS)
    pieces = jnp.concatenate([memory_keys[0], memory_values[0]], axis=0)
    spread = exchange(pieces.reshape(DP, PIECE, COLS))
    mem = exchange(reorder(new_owner, spread)).reshape(2 * MEM, COLS)
    bias = jnp.pad(rel_bias, ((0, 8 - HEADS), (0, 0)))
    prob_seg, seg_out, table = segment(
        seg_queries, seg_keys, seg_values, bias, gain
    )
    attn, prob_mem, factor_mem, factor_seg, stats = forward(
        kept, seg_queries, mem, table, seg_out, cotangent
    )
    others = [
        lax.ppermute(stats, "mp", [(i, (i + step) % 4) for i in range(4)]) for step in (1, 2, 3)
    ]
    attended, og_seg, mem_keys, ds_mem, ds_seg, shares = score_grad(
        [stats] + others, seg_values, mem, cotangent, gain, attn,
        prob_mem, prob_seg, factor_mem, factor_seg,
    )
    query_grad, key_grad, value_grad = input_grad(
        seg_queries, seg_keys, mem_keys, ds_mem, ds_seg, prob_seg, og_seg
    )
    bias_grad, gain_grad = collect(exchange(shares))
    return attended, query_grad, key_grad, value_grad, bias_grad, gain_grad.reshape(COLS)


def solution(mesh):
    row = P("dp", None, "mp")
    return jax.shard_map(
        body,
        mesh=mesh,
        in_specs=(row, row, row, row, row, P(), P(), P("mp", None), P("mp"), row),
        out_specs=(row, row, row, row, P("mp", "dp"), P("mp")),
        check_vma=False,
    )
```

```python
import math

import jax
import jax.numpy as jnp
from jax import lax
from jax.experimental import pallas as pl
from jax.experimental.pallas import tpu as pltpu
from jax.sharding import PartitionSpec as P

DH = 128
BLOCK = 128
HD = 3072
SEG = 256
HALF = SEG // 2
MEM = 256
POS = 512
HEADS = 6
COLS = HEADS * DH
DP = 64
PIECE = (2 * MEM) // DP
LOG2E = math.log2(math.e)
SCALE = DH ** (-0.5)
FACTOR = SCALE * LOG2E
GROUP = 3
CHUNK = 16
LIMIT = 16
NT = (((1,), (1,)), ((), ()))
NN = (((1,), (0,)), ((), ()))
TN = (((0,), (0,)), ((), ()))


def dot(a, b, dims):
    return lax.dot_general(a, b, dims, preferred_element_type=jnp.float32)


def roll(x, shift):
    shift = shift % x.shape[1]
    return x if shift == 0 else pltpu.roll(x, shift, axis=1)


def reverse_lanes(x):
    rows, width = x.shape
    index = 127 - lax.broadcasted_iota(jnp.int32, (rows, 128), 1)
    parts = [
        jnp.take_along_axis(x[:, start : start + 128], index, axis=1)
        for start in range(width - 128, -1, -128)
    ]
    return jnp.concatenate(parts, axis=1)


def by_distance(x):
    return roll(reverse_lanes(x), -255)


def stagger(x, unit):
    row = lax.broadcasted_iota(jnp.int32, x.shape, 0)
    for bit in (1, 2, 4):
        x = jnp.where((row & bit) != 0, roll(x, bit * unit), x)
    return x


def bias_rows(table, head):
    base = stagger(jnp.broadcast_to(table[head : head + 1], (8, POS)), 1)
    return jnp.concatenate([roll(base, 8 * group) for group in range(SEG // 8)], axis=0)


def diagonal_row(score_grad):
    level = [score_grad[8 * g : 8 * g + 8] for g in range(SEG // 8)]
    while len(level) > 1:
        half = len(level) // 2
        level = [level[k] + roll(level[k + half], -8 * half) for k in range(half)]
    return jnp.sum(stagger(level[0], -1), axis=0, keepdims=True)


def reorder_kernel(owner_ref, in_ref, out_ref, held_ref, source_ref, sem):
    for slot in range(DP):
        source_ref[owner_ref[slot]] = slot
    copies = []
    for part in range(DP // CHUNK):
        for dest in range(CHUNK * part, CHUNK * part + CHUNK):
            held_ref[dest] = in_ref[source_ref[dest]]
        rows = pl.ds(CHUNK * part, CHUNK)
        copy = pltpu.make_async_copy(held_ref.at[rows], out_ref.at[rows], sem.at[part])
        copy.start()
        copies.append(copy)
    for copy in copies:
        copy.wait()


def reorder(new_owner, pieces):
    return pl.pallas_call(
        reorder_kernel,
        out_shape=pltpu.HBM(pieces.shape, pieces.dtype),
        in_specs=[
            pl.BlockSpec(memory_space=pltpu.SMEM),
            pl.BlockSpec(memory_space=pltpu.VMEM),
        ],
        out_specs=pl.BlockSpec(memory_space=pl.ANY),
        scratch_shapes=[
            pltpu.VMEM(pieces.shape, pieces.dtype),
            pltpu.SMEM((DP,), jnp.int32),
            pltpu.SemaphoreType.DMA((DP // CHUNK,)),
        ],
        name="reorder",
    )(new_owner, near(pieces))


def segment_kernel(
    q_ref, ks_ref, vs_ref, bias_ref, gain_ref, prob_ref, out_ref, table_ref
):
    col = lax.broadcasted_iota(jnp.int32, (SEG, SEG), 1)
    row = lax.broadcasted_iota(jnp.int32, (SEG, SEG), 0)
    lane = lax.broadcasted_iota(jnp.int32, (SEG, DH), 1)
    rows = jnp.zeros((SEG, DH), jnp.float32)
    table = by_distance(bias_ref[...] * LOG2E)
    for g in range(HEADS):
        cols = slice(DH * g, DH * g + DH)
        bias = bias_rows(table, g)
        table_ref[HALF * g : HALF * g + HALF] = jnp.concatenate(
            [bias[HALF:, :DH], bias[:HALF, :MEM]], axis=1
        )
        scores = dot(q_ref[0, :, cols], ks_ref[0, :, cols], NT) * FACTOR
        scores = jnp.where(col <= row, scores + bias[:, MEM:], -1e30)
        top = jnp.max(scores, axis=1, keepdims=True)
        prob = jnp.exp2(scores - top)
        total = jnp.sum(prob, axis=1, keepdims=True)
        prob = (prob * (1.0 / total)).astype(jnp.bfloat16)
        prob_ref[g] = prob
        out_ref[g] = dot(prob, vs_ref[0, :, cols], NN).astype(jnp.bfloat16)
        rows = jnp.where(lane == g, top + jnp.log2(total), rows)
    table_ref[HALF * HEADS : HALF * HEADS + 8, :SEG] = rows.T[:8]
    for g in range(0, HEADS, 3):
        row = HALF * HEADS + 8 + g // 3
        table_ref[row : row + 1] = gain_ref[:, DH * g : DH * g + 3 * DH]


def forward_kernel(
    kept_ref, q_ref, mem_ref, table_ref, seg_out_hbm, cot_hbm,
    out_ref, prob_ref, factor_mem_ref, factor_seg_ref, stats_ref,
    seg_out_ref, cot_ref, sem,
):
    copies = (
        pltpu.make_async_copy(seg_out_hbm, seg_out_ref, sem.at[0]),
        pltpu.make_async_copy(cot_hbm.at[0], cot_ref, sem.at[1]),
    )
    for copy in copies:
        copy.start()
    ones = jnp.ones((MEM, DH), jnp.bfloat16)
    seg_row = table_ref[HALF * HEADS : HALF * HEADS + 8, :SEG]
    both_kept = jnp.full((SEG, BLOCK), kept_ref[0], jnp.int32) > 1
    for g in range(HEADS):
        cols = slice(DH * g, DH * g + DH)
        scores = dot(q_ref[0, :, cols], mem_ref[:MEM, cols], NT) * FACTOR
        bias = table_ref[HALF * g : HALF * g + HALF]
        scores = scores + jnp.concatenate([bias[:, DH:], bias[:, :MEM]], axis=0)
        scores = jnp.concatenate([jnp.where(both_kept, scores[:, :BLOCK], -1e30), scores[:, BLOCK:]], axis=1)
        seg_top = jnp.broadcast_to(seg_row[g : g + 1], (DH, SEG)).T
        top = jnp.maximum(jnp.max(scores, axis=1, keepdims=True), seg_top)
        prob = jnp.exp2(scores - jnp.concatenate([top, top], axis=1)).astype(jnp.bfloat16)
        prob_ref[g] = prob
        both = dot(prob, jnp.concatenate([mem_ref[MEM:, cols], ones], axis=1), NN)
        shrink = jnp.exp2(seg_top - top)
        inverse = 1.0 / (both[:, DH:] + shrink)
        factor_mem_ref[:, cols] = inverse
        factor_seg_ref[:, cols] = shrink * inverse
        out_ref[:, cols] = both[:, :DH] * inverse
    for copy in copies:
        copy.wait()
    square = cross = None
    for g in range(HEADS):
        cols = slice(DH * g, DH * g + DH)
        out = out_ref[:, cols] + seg_out_ref[g].astype(jnp.float32) * factor_seg_ref[:, cols]
        out_ref[:, cols] = out
        row = HALF * HEADS + 8 + g // 3
        gain = table_ref[row : row + 1, DH * (g % 3) : DH * (g % 3) + DH]
        part = cot_ref[:, cols].astype(jnp.float32) * gain * out
        square = out * out if g == 0 else square + out * out
        cross = part if g == 0 else cross + part
    stats_ref[...] = jnp.zeros((8, SEG), jnp.float32)
    stats_ref[0:1, :] = jnp.sum(square.T, axis=0, keepdims=True)
    stats_ref[1:2, :] = jnp.sum(cross.T, axis=0, keepdims=True)


def score_grad_kernel(
    stats0_ref, stats1_ref, stats2_ref, stats3_ref,
    mem_ref, cot_ref, gain_ref, attn_ref, prob_mem_ref, prob_seg_ref,
    factor_mem_ref, factor_seg_ref, vs_hbm,
    attended_hbm, og_seg_hbm, keys_hbm, ds_mem_ref, ds_seg_ref, share_ref,
    attended_ref, og_seg_ref, og_mem_ref, less_ref, vs_ref, sem,
):
    values_copy = pltpu.make_async_copy(vs_hbm.at[0], vs_ref, sem.at[0])
    values_copy.start()
    keys_copy = pltpu.make_async_copy(mem_ref.at[pl.ds(0, MEM)], keys_hbm, sem.at[1])
    keys_copy.start()
    stats = (stats0_ref[...] + stats1_ref[...]) + (stats2_ref[...] + stats3_ref[...])
    inv = lax.rsqrt(stats[0:1] / HD + 1e-06)
    coef = inv * inv * inv * stats[1:2] / HD
    inv = jnp.broadcast_to(inv, (DH, SEG)).T
    coef = jnp.broadcast_to(coef, (DH, SEG)).T
    gains = []
    for g in range(HEADS):
        cols = slice(DH * g, DH * g + DH)
        attn = attn_ref[:, cols]
        gain = gain_ref[:, cols]
        upstream = cot_ref[0, :, cols].astype(jnp.float32)
        normed = attn * inv
        attended_ref[:, cols] = (normed * gain).astype(jnp.bfloat16)
        gains.append(jnp.sum(upstream * normed, axis=0, keepdims=True))
        out_grad = inv * (upstream * gain) - attn * coef
        less_ref[g] = jnp.broadcast_to(
            jnp.sum(out_grad * attn, axis=1, keepdims=True), (SEG, DH)
        )
        og_mem_ref[g] = (out_grad * factor_mem_ref[:, cols]).astype(jnp.bfloat16)
        og_seg_ref[g] = (out_grad * factor_seg_ref[:, cols]).astype(jnp.bfloat16)
    copies = (
        pltpu.make_async_copy(attended_ref, attended_hbm.at[0], sem.at[2]),
        pltpu.make_async_copy(og_seg_ref, og_seg_hbm, sem.at[3]),
    )
    for copy in copies:
        copy.start()
    values_copy.wait()
    diagonals = []
    for g in range(HEADS):
        cols = slice(DH * g, DH * g + DH)
        less_mem = less_ref[g] * factor_mem_ref[:, cols]
        less_seg = less_ref[g] * factor_seg_ref[:, cols]
        dp_mem = dot(og_mem_ref[g], mem_ref[MEM:, cols], NT)
        dp_seg = dot(og_seg_ref[g], vs_ref[:, cols], NT)
        dp_mem = dp_mem - jnp.concatenate([less_mem, less_mem], axis=1)
        dp_seg = dp_seg - jnp.concatenate([less_seg, less_seg], axis=1)
        ds_mem = prob_mem_ref[g].astype(jnp.float32) * dp_mem
        ds_seg = prob_seg_ref[g].astype(jnp.float32) * dp_seg
        ds_mem_ref[g] = ds_mem.astype(jnp.bfloat16)
        ds_seg_ref[g] = ds_seg.astype(jnp.bfloat16)
        diagonals.append(diagonal_row(jnp.concatenate([ds_mem, ds_seg], axis=1)))

    pad = [jnp.zeros((2, DH), jnp.float32)]
    gains = jnp.concatenate(gains + pad, axis=0)
    diagonals = jnp.concatenate(diagonals + [jnp.zeros((2, POS), jnp.float32)], axis=0)
    bias = stagger(by_distance(diagonals), 8)
    bias = jnp.concatenate([bias, bias[:, :128]], axis=1)
    lane = lax.broadcasted_iota(jnp.int32, (8, DH), 1)
    row = lax.broadcasted_iota(jnp.int32, (8, DH), 0)
    own = (lane >= 8 * row) & (lane < 8 * row + 8) & (row < HEADS)
    for dest in range(DP):
        start, shift = divmod(8 * dest, 128)
        here = bias[:, 128 * start : 128 * start + 128]
        after = bias[:, 128 * start + 128 : 128 * start + 256]
        part = jnp.where(lane < 128 - shift, roll(here, -shift), roll(after, -shift))
        part = jnp.sum(jnp.where(own, part, 0.0), axis=0, keepdims=True)
        share_ref[dest] = jnp.where(row == HEADS, part, gains).astype(share_ref.dtype)
    keys_copy.wait()
    for copy in copies:
        copy.wait()


def input_grad_kernel(
    q_ref, ks_ref, mem_ref, ds_mem_ref, ds_seg_ref, prob_seg_ref, og_seg_ref,
    dq_ref, dk_ref, dv_ref,
):
    for g in range(GROUP):
        cols = slice(DH * g, DH * g + DH)
        ds_seg = ds_seg_ref[g]
        dq = dot(ds_mem_ref[g], mem_ref[:, cols], NN) + dot(ds_seg, ks_ref[0, :, cols], NN)
        dq_ref[0, :, cols] = (dq * SCALE).astype(jnp.bfloat16)
        dk_ref[0, :, cols] = (dot(ds_seg, q_ref[0, :, cols], TN) * SCALE).astype(jnp.bfloat16)
        dv_ref[0, :, cols] = dot(prob_seg_ref[g], og_seg_ref[g], TN).astype(jnp.bfloat16)


TOKENS = jax.ShapeDtypeStruct((1, SEG, COLS), jnp.bfloat16)
COLUMNS = jax.ShapeDtypeStruct((SEG, COLS), jnp.float32)
HEAD_COLUMNS = jax.ShapeDtypeStruct((HEADS, SEG, DH), jnp.float32)
HEAD_COLUMNS_B = jax.ShapeDtypeStruct((HEADS, SEG, DH), jnp.bfloat16)
TABLE = jax.ShapeDtypeStruct((HEADS * HALF + 16, MEM + DH), jnp.float32)
STATS = jax.ShapeDtypeStruct((8, SEG), jnp.float32)
KEYS = jax.ShapeDtypeStruct((MEM, COLS), jnp.bfloat16)
SHARES = jax.ShapeDtypeStruct((DP, 8, DH), jnp.bfloat16)
SQUARES_B = jax.ShapeDtypeStruct((HEADS, SEG, SEG), jnp.bfloat16)


def far(x):
    return pltpu.with_memory_space_constraint(x, pltpu.HBM)


def far_out(shape):
    return pltpu.HBM(shape.shape, shape.dtype)


def near(x):
    return pltpu.with_memory_space_constraint(x, pltpu.VMEM)


def near_out(shape):
    return pltpu.VMEM(shape.shape, shape.dtype)


def near_call(kernel, scalars, ins, far_ins, outs, far_outs, tail=(), scratch=()):
    spec = pl.BlockSpec(memory_space=pltpu.VMEM)
    any_spec = pl.BlockSpec(memory_space=pl.ANY)
    return pl.pallas_call(
        kernel,
        in_specs=[pl.BlockSpec(memory_space=pltpu.SMEM)] * len(scalars)
        + [spec] * len(ins)
        + [any_spec] * len(far_ins),
        out_shape=tuple(far_out(x) for x in far_outs) + tuple(outs) + tuple(tail),
        out_specs=(any_spec,) * len(far_outs) + (spec,) * (len(outs) + len(tail)),
        scratch_shapes=scratch,
        compiler_params=pltpu.CompilerParams(vmem_limit_bytes=LIMIT << 20),
        name=kernel.__name__,
    )(*scalars, *[near(x) for x in ins], *[far(x) for x in far_ins])


def segment(q, ks, vs, bias, gain):
    spec = pl.BlockSpec(memory_space=pltpu.VMEM)
    return pl.pallas_call(
        segment_kernel,
        in_specs=[spec] * 5,
        out_shape=(
            far_out(SQUARES_B), far_out(HEAD_COLUMNS_B), near_out(TABLE),
        ),
        out_specs=(spec,) * 3,
        compiler_params=pltpu.CompilerParams(vmem_limit_bytes=LIMIT << 20),
        name="segment_kernel",
    )(far(q), far(ks), far(vs), bias, far(gain))


def forward(kept, q, mem, table, seg_out, cot):
    return near_call(
        forward_kernel,
        (kept,),
        (q, mem, table),
        (seg_out, cot),
        [near_out(x) for x in (COLUMNS, SQUARES_B, COLUMNS, COLUMNS, STATS)],
        (),
        scratch=[
            pltpu.VMEM((HEADS, SEG, DH), jnp.bfloat16),
            pltpu.VMEM((SEG, COLS), jnp.bfloat16),
            pltpu.SemaphoreType.DMA((2,)),
        ],
    )


def score_grad(stats, vs, mem, cot, gain, attn, prob_mem, prob_seg, factor_mem, factor_seg):
    return near_call(
        score_grad_kernel,
        (),
        (*stats, mem, cot, gain, attn, prob_mem, prob_seg, factor_mem, factor_seg),
        (vs,),
        [near_out(SQUARES_B), near_out(SQUARES_B), far_out(SHARES)],
        (TOKENS, HEAD_COLUMNS_B, KEYS),
        scratch=[
            pltpu.VMEM((SEG, COLS), jnp.bfloat16),
            pltpu.VMEM((HEADS, SEG, DH), jnp.bfloat16),
            pltpu.VMEM((HEADS, SEG, DH), jnp.bfloat16),
            pltpu.VMEM((HEADS, SEG, DH), jnp.float32),
            pltpu.VMEM((SEG, COLS), jnp.bfloat16),
            pltpu.SemaphoreType.DMA((4,)),
        ],
    )


def input_grad(q, ks, keys, ds_mem, ds_seg, prob_seg, og_seg):
    tokens = pl.BlockSpec((1, SEG, DH * GROUP), lambda h: (0, 0, h))
    squares = pl.BlockSpec((GROUP, SEG, SEG), lambda h: (h, 0, 0))
    return pl.pallas_call(
        input_grad_kernel,
        grid=(HEADS // GROUP,),
        in_specs=[
            tokens,
            tokens,
            pl.BlockSpec((MEM, DH * GROUP), lambda h: (0, h)),
            squares,
            squares,
            squares,
            pl.BlockSpec((GROUP, SEG, DH), lambda h: (h, 0, 0)),
        ],
        out_shape=tuple(far_out(TOKENS) for _ in range(3)),
        out_specs=(tokens,) * 3,
        compiler_params=pltpu.CompilerParams(vmem_limit_bytes=LIMIT << 20),
        name="input_grad_kernel",
    )(far(q), far(ks), far(keys), near(ds_mem), near(ds_seg), far(prob_seg), far(og_seg))


def collect_kernel(share_ref, bias_ref, gain_ref):
    total = jnp.sum(share_ref[...].astype(jnp.float32), axis=0)
    gain_ref[...] = total[:HEADS]
    bias = stagger(jnp.broadcast_to(total[HEADS : HEADS + 1], (8, DH)), -8)
    bias_ref[...] = bias[:HEADS, :8]


def collect(shares):
    return pl.pallas_call(
        collect_kernel,
        in_specs=[pl.BlockSpec(memory_space=pltpu.VMEM)],
        out_shape=(
            pltpu.HBM((HEADS, 8), jnp.float32),
            pltpu.HBM((HEADS, DH), jnp.float32),
        ),
        name="collect",
    )(near(shares))


def exchange(x):
    return lax.all_to_all(x, "dp", split_axis=0, concat_axis=0, tiled=True)


def body(
    seg_queries, seg_keys, seg_values, memory_keys, memory_values,
    new_owner, kept_blocks, rel_bias, norm_gain, cotangent,
):
    own_index = lax.axis_index("dp")
    kept = jnp.sum(jnp.where(new_owner == own_index, kept_blocks, 0)).reshape(1)
    gain = norm_gain.reshape(1, COLS)
    pieces = jnp.concatenate([memory_keys[0], memory_values[0]], axis=0)
    spread = exchange(pieces.reshape(DP, PIECE, COLS))
    mem = exchange(reorder(new_owner, spread)).reshape(2 * MEM, COLS)
    bias = jnp.pad(rel_bias, ((0, 8 - HEADS), (0, 0)))
    prob_seg, seg_out, table = segment(
        seg_queries, seg_keys, seg_values, bias, gain
    )
    attn, prob_mem, factor_mem, factor_seg, stats = forward(
        kept, seg_queries, mem, table, seg_out, cotangent
    )
    others = [
        lax.ppermute(stats, "mp", [(i, (i + step) % 4) for i in range(4)]) for step in (1, 2, 3)
    ]
    attended, og_seg, mem_keys, ds_mem, ds_seg, shares = score_grad(
        [stats] + others, seg_values, mem, cotangent, gain, attn,
        prob_mem, prob_seg, factor_mem, factor_seg,
    )
    query_grad, key_grad, value_grad = input_grad(
        seg_queries, seg_keys, mem_keys, ds_mem, ds_seg, prob_seg, og_seg
    )
    bias_grad, gain_grad = collect(exchange(shares))
    return attended, query_grad, key_grad, value_grad, bias_grad, gain_grad.reshape(COLS)


def solution(mesh):
    row = P("dp", None, "mp")
    return jax.shard_map(
        body,
        mesh=mesh,
        in_specs=(row, row, row, row, row, P(), P(), P("mp", None), P("mp"), row),
        out_specs=(row, row, row, row, P("mp", "dp"), P("mp")),
        check_vma=False,
    )
```

```python
import math

import jax
import jax.numpy as jnp
from jax import lax
from jax.experimental import pallas as pl
from jax.experimental.pallas import tpu as pltpu
from jax.sharding import PartitionSpec as P

DH = 128
BLOCK = 128
HD = 3072
SEG = 256
HALF = SEG // 2
MEM = 256
POS = 512
HEADS = 6
COLS = HEADS * DH
DP = 64
PIECE = (2 * MEM) // DP
LOG2E = math.log2(math.e)
SCALE = DH ** (-0.5)
FACTOR = SCALE * LOG2E
GROUP = 3
CHUNK = 32
LIMIT = 16
NT = (((1,), (1,)), ((), ()))
NN = (((1,), (0,)), ((), ()))
TN = (((0,), (0,)), ((), ()))


def dot(a, b, dims):
    return lax.dot_general(a, b, dims, preferred_element_type=jnp.float32)


def roll(x, shift):
    shift = shift % x.shape[1]
    return x if shift == 0 else pltpu.roll(x, shift, axis=1)


def reverse_lanes(x):
    rows, width = x.shape
    index = 127 - lax.broadcasted_iota(jnp.int32, (rows, 128), 1)
    parts = [
        jnp.take_along_axis(x[:, start : start + 128], index, axis=1)
        for start in range(width - 128, -1, -128)
    ]
    return jnp.concatenate(parts, axis=1)


def by_distance(x):
    return roll(reverse_lanes(x), -255)


def stagger(x, unit):
    row = lax.broadcasted_iota(jnp.int32, x.shape, 0)
    for bit in (1, 2, 4):
        x = jnp.where((row & bit) != 0, roll(x, bit * unit), x)
    return x


def bias_rows(table, head):
    base = stagger(jnp.broadcast_to(table[head : head + 1], (8, POS)), 1)
    return jnp.concatenate([roll(base, 8 * group) for group in range(SEG // 8)], axis=0)


def diagonal_row(score_grad):
    level = [score_grad[8 * g : 8 * g + 8] for g in range(SEG // 8)]
    while len(level) > 1:
        half = len(level) // 2
        level = [level[k] + roll(level[k + half], -8 * half) for k in range(half)]
    return jnp.sum(stagger(level[0], -1), axis=0, keepdims=True)


def reorder_kernel(owner_ref, in_ref, out_ref, held_ref, source_ref, sem):
    for slot in range(DP):
        source_ref[owner_ref[slot]] = slot
    copies = []
    for part in range(DP // CHUNK):
        for dest in range(CHUNK * part, CHUNK * part + CHUNK):
            held_ref[dest] = in_ref[source_ref[dest]]
        rows = pl.ds(CHUNK * part, CHUNK)
        copy = pltpu.make_async_copy(held_ref.at[rows], out_ref.at[rows], sem.at[part])
        copy.start()
        copies.append(copy)
    for copy in copies:
        copy.wait()


def reorder(new_owner, pieces):
    return pl.pallas_call(
        reorder_kernel,
        out_shape=pltpu.HBM(pieces.shape, pieces.dtype),
        in_specs=[
            pl.BlockSpec(memory_space=pltpu.SMEM),
            pl.BlockSpec(memory_space=pltpu.VMEM),
        ],
        out_specs=pl.BlockSpec(memory_space=pl.ANY),
        scratch_shapes=[
            pltpu.VMEM(pieces.shape, pieces.dtype),
            pltpu.SMEM((DP,), jnp.int32),
            pltpu.SemaphoreType.DMA((DP // CHUNK,)),
        ],
        name="reorder",
    )(new_owner, near(pieces))


def segment_kernel(
    q_ref, ks_ref, vs_ref, bias_ref, gain_ref, prob_ref, out_ref, table_ref
):
    col = lax.broadcasted_iota(jnp.int32, (SEG, SEG), 1)
    row = lax.broadcasted_iota(jnp.int32, (SEG, SEG), 0)
    lane = lax.broadcasted_iota(jnp.int32, (SEG, DH), 1)
    rows = jnp.zeros((SEG, DH), jnp.float32)
    table = by_distance(bias_ref[...] * LOG2E)
    for g in range(HEADS):
        cols = slice(DH * g, DH * g + DH)
        bias = bias_rows(table, g)
        table_ref[HALF * g : HALF * g + HALF] = jnp.concatenate(
            [bias[HALF:, :DH], bias[:HALF, :MEM]], axis=1
        )
        scores = dot(q_ref[0, :, cols], ks_ref[0, :, cols], NT) * FACTOR
        scores = jnp.where(col <= row, scores + bias[:, MEM:], -1e30)
        top = jnp.max(scores, axis=1, keepdims=True)
        prob = jnp.exp2(scores - top)
        total = jnp.sum(prob, axis=1, keepdims=True)
        prob = (prob * (1.0 / total)).astype(jnp.bfloat16)
        prob_ref[g] = prob
        out_ref[g] = dot(prob, vs_ref[0, :, cols], NN)
        rows = jnp.where(lane == g, top + jnp.log2(total), rows)
    table_ref[HALF * HEADS : HALF * HEADS + 8, :SEG] = rows.T[:8]
    for g in range(0, HEADS, 3):
        row = HALF * HEADS + 8 + g // 3
        table_ref[row : row + 1] = gain_ref[:, DH * g : DH * g + 3 * DH]


def forward_kernel(
    kept_ref, q_ref, mem_ref, table_ref, seg_out_hbm, cot_hbm,
    out_ref, prob_ref, factor_mem_ref, factor_seg_ref, stats_ref,
    seg_out_ref, cot_ref, sem,
):
    copies = (
        pltpu.make_async_copy(seg_out_hbm, seg_out_ref, sem.at[0]),
        pltpu.make_async_copy(cot_hbm.at[0], cot_ref, sem.at[1]),
    )
    for copy in copies:
        copy.start()
    ones = jnp.ones((MEM, DH), jnp.bfloat16)
    seg_row = table_ref[HALF * HEADS : HALF * HEADS + 8, :SEG]
    both_kept = jnp.full((SEG, BLOCK), kept_ref[0], jnp.int32) > 1
    for g in range(HEADS):
        cols = slice(DH * g, DH * g + DH)
        scores = dot(q_ref[0, :, cols], mem_ref[:MEM, cols], NT) * FACTOR
        bias = table_ref[HALF * g : HALF * g + HALF]
        scores = scores + jnp.concatenate([bias[:, DH:], bias[:, :MEM]], axis=0)
        scores = jnp.concatenate([jnp.where(both_kept, scores[:, :BLOCK], -1e30), scores[:, BLOCK:]], axis=1)
        seg_top = jnp.broadcast_to(seg_row[g : g + 1], (DH, SEG)).T
        top = jnp.maximum(jnp.max(scores, axis=1, keepdims=True), seg_top)
        prob = jnp.exp2(scores - jnp.concatenate([top, top], axis=1)).astype(jnp.bfloat16)
        prob_ref[g] = prob
        both = dot(prob, jnp.concatenate([mem_ref[MEM:, cols], ones], axis=1), NN)
        shrink = jnp.exp2(seg_top - top)
        inverse = 1.0 / (both[:, DH:] + shrink)
        factor_mem_ref[:, cols] = inverse
        factor_seg_ref[:, cols] = shrink * inverse
        out_ref[:, cols] = both[:, :DH] * inverse
    for copy in copies:
        copy.wait()
    square = cross = None
    for g in range(HEADS):
        cols = slice(DH * g, DH * g + DH)
        out = out_ref[:, cols] + seg_out_ref[g] * factor_seg_ref[:, cols]
        out_ref[:, cols] = out
        row = HALF * HEADS + 8 + g // 3
        gain = table_ref[row : row + 1, DH * (g % 3) : DH * (g % 3) + DH]
        part = cot_ref[:, cols].astype(jnp.float32) * gain * out
        square = out * out if g == 0 else square + out * out
        cross = part if g == 0 else cross + part
    stats_ref[...] = jnp.zeros((8, SEG), jnp.float32)
    stats_ref[0:1, :] = jnp.sum(square.T, axis=0, keepdims=True)
    stats_ref[1:2, :] = jnp.sum(cross.T, axis=0, keepdims=True)


def score_grad_kernel(
    stats0_ref, stats1_ref, stats2_ref, stats3_ref,
    mem_ref, cot_ref, gain_ref, attn_ref, prob_mem_ref, prob_seg_ref,
    factor_mem_ref, factor_seg_ref, vs_hbm,
    attended_hbm, og_seg_hbm, keys_hbm, ds_mem_ref, ds_seg_ref, share_ref,
    attended_ref, og_seg_ref, og_mem_ref, less_ref, vs_ref, sem,
):
    values_copy = pltpu.make_async_copy(vs_hbm.at[0], vs_ref, sem.at[0])
    values_copy.start()
    keys_copy = pltpu.make_async_copy(mem_ref.at[pl.ds(0, MEM)], keys_hbm, sem.at[1])
    keys_copy.start()
    stats = (stats0_ref[...] + stats1_ref[...]) + (stats2_ref[...] + stats3_ref[...])
    inv = lax.rsqrt(stats[0:1] / HD + 1e-06)
    coef = inv * inv * inv * stats[1:2] / HD
    inv = jnp.broadcast_to(inv, (DH, SEG)).T
    coef = jnp.broadcast_to(coef, (DH, SEG)).T
    gains = []
    for g in range(HEADS):
        cols = slice(DH * g, DH * g + DH)
        attn = attn_ref[:, cols]
        gain = gain_ref[:, cols]
        upstream = cot_ref[0, :, cols].astype(jnp.float32)
        normed = attn * inv
        attended_ref[:, cols] = (normed * gain).astype(jnp.bfloat16)
        gains.append(jnp.sum(upstream * normed, axis=0, keepdims=True))
        out_grad = inv * (upstream * gain) - attn * coef
        less_ref[g] = jnp.broadcast_to(
            jnp.sum(out_grad * attn, axis=1, keepdims=True), (SEG, DH)
        )
        og_mem_ref[g] = (out_grad * factor_mem_ref[:, cols]).astype(jnp.bfloat16)
        og_seg_ref[g] = (out_grad * factor_seg_ref[:, cols]).astype(jnp.bfloat16)
    copies = (
        pltpu.make_async_copy(attended_ref, attended_hbm.at[0], sem.at[2]),
        pltpu.make_async_copy(og_seg_ref, og_seg_hbm, sem.at[3]),
    )
    for copy in copies:
        copy.start()
    values_copy.wait()
    diagonals = []
    for g in range(HEADS):
        cols = slice(DH * g, DH * g + DH)
        less_mem = less_ref[g] * factor_mem_ref[:, cols]
        less_seg = less_ref[g] * factor_seg_ref[:, cols]
        dp_mem = dot(og_mem_ref[g], mem_ref[MEM:, cols], NT)
        dp_seg = dot(og_seg_ref[g], vs_ref[:, cols], NT)
        dp_mem = dp_mem - jnp.concatenate([less_mem, less_mem], axis=1)
        dp_seg = dp_seg - jnp.concatenate([less_seg, less_seg], axis=1)
        ds_mem = prob_mem_ref[g].astype(jnp.float32) * dp_mem
        ds_seg = prob_seg_ref[g].astype(jnp.float32) * dp_seg
        ds_mem_ref[g] = ds_mem.astype(jnp.bfloat16)
        ds_seg_ref[g] = ds_seg.astype(jnp.bfloat16)
        diagonals.append(diagonal_row(jnp.concatenate([ds_mem, ds_seg], axis=1)))

    pad = [jnp.zeros((2, DH), jnp.float32)]
    gains = jnp.concatenate(gains + pad, axis=0)
    diagonals = jnp.concatenate(diagonals + [jnp.zeros((2, POS), jnp.float32)], axis=0)
    bias = stagger(by_distance(diagonals), 8)
    bias = jnp.concatenate([bias, bias[:, :128]], axis=1)
    lane = lax.broadcasted_iota(jnp.int32, (8, DH), 1)
    row = lax.broadcasted_iota(jnp.int32, (8, DH), 0)
    own = (lane >= 8 * row) & (lane < 8 * row + 8) & (row < HEADS)
    for dest in range(DP):
        start, shift = divmod(8 * dest, 128)
        here = bias[:, 128 * start : 128 * start + 128]
        after = bias[:, 128 * start + 128 : 128 * start + 256]
        part = jnp.where(lane < 128 - shift, roll(here, -shift), roll(after, -shift))
        part = jnp.sum(jnp.where(own, part, 0.0), axis=0, keepdims=True)
        share_ref[dest] = jnp.where(row == HEADS, part, gains).astype(share_ref.dtype)
    keys_copy.wait()
    for copy in copies:
        copy.wait()


def input_grad_kernel(
    q_ref, ks_ref, mem_ref, ds_mem_ref, ds_seg_ref, prob_seg_ref, og_seg_ref,
    dq_ref, dk_ref, dv_ref,
):
    for g in range(GROUP):
        cols = slice(DH * g, DH * g + DH)
        ds_seg = ds_seg_ref[g]
        dq = dot(ds_mem_ref[g], mem_ref[:, cols], NN) + dot(ds_seg, ks_ref[0, :, cols], NN)
        dq_ref[0, :, cols] = (dq * SCALE).astype(jnp.bfloat16)
        dk_ref[0, :, cols] = (dot(ds_seg, q_ref[0, :, cols], TN) * SCALE).astype(jnp.bfloat16)
        dv_ref[0, :, cols] = dot(prob_seg_ref[g], og_seg_ref[g], TN).astype(jnp.bfloat16)


TOKENS = jax.ShapeDtypeStruct((1, SEG, COLS), jnp.bfloat16)
COLUMNS = jax.ShapeDtypeStruct((SEG, COLS), jnp.float32)
HEAD_COLUMNS = jax.ShapeDtypeStruct((HEADS, SEG, DH), jnp.float32)
HEAD_COLUMNS_B = jax.ShapeDtypeStruct((HEADS, SEG, DH), jnp.bfloat16)
TABLE = jax.ShapeDtypeStruct((HEADS * HALF + 16, MEM + DH), jnp.float32)
STATS = jax.ShapeDtypeStruct((8, SEG), jnp.float32)
KEYS = jax.ShapeDtypeStruct((MEM, COLS), jnp.bfloat16)
SHARES = jax.ShapeDtypeStruct((DP, 8, DH), jnp.bfloat16)
SQUARES_B = jax.ShapeDtypeStruct((HEADS, SEG, SEG), jnp.bfloat16)


def far(x):
    return pltpu.with_memory_space_constraint(x, pltpu.HBM)


def far_out(shape):
    return pltpu.HBM(shape.shape, shape.dtype)


def near(x):
    return pltpu.with_memory_space_constraint(x, pltpu.VMEM)


def near_out(shape):
    return pltpu.VMEM(shape.shape, shape.dtype)


def near_call(kernel, scalars, ins, far_ins, outs, far_outs, tail=(), scratch=()):
    spec = pl.BlockSpec(memory_space=pltpu.VMEM)
    any_spec = pl.BlockSpec(memory_space=pl.ANY)
    return pl.pallas_call(
        kernel,
        in_specs=[pl.BlockSpec(memory_space=pltpu.SMEM)] * len(scalars)
        + [spec] * len(ins)
        + [any_spec] * len(far_ins),
        out_shape=tuple(far_out(x) for x in far_outs) + tuple(outs) + tuple(tail),
        out_specs=(any_spec,) * len(far_outs) + (spec,) * (len(outs) + len(tail)),
        scratch_shapes=scratch,
        compiler_params=pltpu.CompilerParams(vmem_limit_bytes=LIMIT << 20),
        name=kernel.__name__,
    )(*scalars, *[near(x) for x in ins], *[far(x) for x in far_ins])


def segment(q, ks, vs, bias, gain):
    spec = pl.BlockSpec(memory_space=pltpu.VMEM)
    return pl.pallas_call(
        segment_kernel,
        in_specs=[spec] * 5,
        out_shape=(
            far_out(SQUARES_B), far_out(HEAD_COLUMNS), near_out(TABLE),
        ),
        out_specs=(spec,) * 3,
        compiler_params=pltpu.CompilerParams(vmem_limit_bytes=LIMIT << 20),
        name="segment_kernel",
    )(far(q), far(ks), far(vs), bias, far(gain))


def forward(kept, q, mem, table, seg_out, cot):
    return near_call(
        forward_kernel,
        (kept,),
        (q, mem, table),
        (seg_out, cot),
        [near_out(x) for x in (COLUMNS, SQUARES_B, COLUMNS, COLUMNS, STATS)],
        (),
        scratch=[
            pltpu.VMEM((HEADS, SEG, DH), jnp.float32),
            pltpu.VMEM((SEG, COLS), jnp.bfloat16),
            pltpu.SemaphoreType.DMA((2,)),
        ],
    )


def score_grad(stats, vs, mem, cot, gain, attn, prob_mem, prob_seg, factor_mem, factor_seg):
    return near_call(
        score_grad_kernel,
        (),
        (*stats, mem, cot, gain, attn, prob_mem, prob_seg, factor_mem, factor_seg),
        (vs,),
        [near_out(SQUARES_B), near_out(SQUARES_B), far_out(SHARES)],
        (TOKENS, HEAD_COLUMNS_B, KEYS),
        scratch=[
            pltpu.VMEM((SEG, COLS), jnp.bfloat16),
            pltpu.VMEM((HEADS, SEG, DH), jnp.bfloat16),
            pltpu.VMEM((HEADS, SEG, DH), jnp.bfloat16),
            pltpu.VMEM((HEADS, SEG, DH), jnp.float32),
            pltpu.VMEM((SEG, COLS), jnp.bfloat16),
            pltpu.SemaphoreType.DMA((4,)),
        ],
    )


def input_grad(q, ks, keys, ds_mem, ds_seg, prob_seg, og_seg):
    tokens = pl.BlockSpec((1, SEG, DH * GROUP), lambda h: (0, 0, h))
    squares = pl.BlockSpec((GROUP, SEG, SEG), lambda h: (h, 0, 0))
    return pl.pallas_call(
        input_grad_kernel,
        grid=(HEADS // GROUP,),
        in_specs=[
            tokens,
            tokens,
            pl.BlockSpec((MEM, DH * GROUP), lambda h: (0, h)),
            squares,
            squares,
            squares,
            pl.BlockSpec((GROUP, SEG, DH), lambda h: (h, 0, 0)),
        ],
        out_shape=tuple(far_out(TOKENS) for _ in range(3)),
        out_specs=(tokens,) * 3,
        compiler_params=pltpu.CompilerParams(vmem_limit_bytes=LIMIT << 20),
        name="input_grad_kernel",
    )(far(q), far(ks), far(keys), near(ds_mem), near(ds_seg), far(prob_seg), far(og_seg))


def collect_kernel(share_ref, bias_ref, gain_ref):
    total = jnp.sum(share_ref[...].astype(jnp.float32), axis=0)
    gain_ref[...] = total[:HEADS]
    bias = stagger(jnp.broadcast_to(total[HEADS : HEADS + 1], (8, DH)), -8)
    bias_ref[...] = bias[:HEADS, :8]


def collect(shares):
    return pl.pallas_call(
        collect_kernel,
        in_specs=[pl.BlockSpec(memory_space=pltpu.VMEM)],
        out_shape=(
            pltpu.HBM((HEADS, 8), jnp.float32),
            pltpu.HBM((HEADS, DH), jnp.float32),
        ),
        name="collect",
    )(near(shares))


def exchange(x):
    return lax.all_to_all(x, "dp", split_axis=0, concat_axis=0, tiled=True)


def body(
    seg_queries, seg_keys, seg_values, memory_keys, memory_values,
    new_owner, kept_blocks, rel_bias, norm_gain, cotangent,
):
    own_index = lax.axis_index("dp")
    kept = jnp.sum(jnp.where(new_owner == own_index, kept_blocks, 0)).reshape(1)
    gain = norm_gain.reshape(1, COLS)
    pieces = jnp.concatenate([memory_keys[0], memory_values[0]], axis=0)
    spread = exchange(pieces.reshape(DP, PIECE, COLS))
    mem = exchange(reorder(new_owner, spread)).reshape(2 * MEM, COLS)
    bias = jnp.pad(rel_bias, ((0, 8 - HEADS), (0, 0)))
    prob_seg, seg_out, table = segment(
        seg_queries, seg_keys, seg_values, bias, gain
    )
    attn, prob_mem, factor_mem, factor_seg, stats = forward(
        kept, seg_queries, mem, table, seg_out, cotangent
    )
    others = [
        lax.ppermute(stats, "mp", [(i, (i + step) % 4) for i in range(4)]) for step in (1, 2, 3)
    ]
    attended, og_seg, mem_keys, ds_mem, ds_seg, shares = score_grad(
        [stats] + others, seg_values, mem, cotangent, gain, attn,
        prob_mem, prob_seg, factor_mem, factor_seg,
    )
    query_grad, key_grad, value_grad = input_grad(
        seg_queries, seg_keys, mem_keys, ds_mem, ds_seg, prob_seg, og_seg
    )
    bias_grad, gain_grad = collect(exchange(shares))
    return attended, query_grad, key_grad, value_grad, bias_grad, gain_grad.reshape(COLS)


def solution(mesh):
    row = P("dp", None, "mp")
    return jax.shard_map(
        body,
        mesh=mesh,
        in_specs=(row, row, row, row, row, P(), P(), P("mp", None), P("mp"), row),
        out_specs=(row, row, row, row, P("mp", "dp"), P("mp")),
        check_vma=False,
    )
```
